32 devices in a mesh: az: 8 (over z, x), rx: 4 (over y, core).
Axes of the slice: x: 2, y: 2, z: 4, core: 2. Of those that a mesh axis runs over, the one named last changes fastest.
Arguments:
- adjoint: float32 [5, 8, 128, 512], P(None, 'az', None, 'rx'), may hold values from -6 to 6
- density: float32 [8, 128, 512], P('az', None, 'rx'), may hold values from 0.6 to 1.4
- velocity: float32 [3, 8, 128, 512], P(None, 'az', None, 'rx'), may hold values from -0.9 to 0.9
- pressure: float32 [8, 128, 512], P('az', None, 'rx'), may hold values from 0.5 to 0.9
- fwh_cell: int32 [8, 4, 256], P('az', 'rx'), may hold values from 0 to 16383
- fwh_bin: int32 [8, 4, 256], P('az', 'rx'), may hold values from 0 to 255
- fwh_weight: float32 [8, 4, 256], P('az', 'rx'), may hold values from -6 to 6
- fwh_count: int32 [8, 4], P('az', 'rx'), may hold values from 1 to 256, as said below
Outputs:
- section: float32 [5, 8, 128, 512], P(None, 'az', None, 'rx')
- signal: float32 [256], P(('az', 'rx'))
The draws below stay inside these ranges and needn't reach their ends.
Inputs may be any that keep to these rules, and one draw needn't show every extreme that they name: `fwh_count`: slots at or after a device's count are unused; some device has all 256 slots live.
All inputs are finite; a program needn't handle non-finite values.
Results may differ from the reference program's by a relative error of at most 0.00017.
Values sent between devices are 32-bit elements; how exact they have to be, the bound alone decides.
No kernel may reach another device: no remote copies, remote signals or barrier semaphores. Data moves between devices by JAX's collectives and lax.ppermute only.
A program may use at most 64 MiB of HBM per device.

```python
import math
import jax
import jax.numpy as jnp
from jax import lax

AZ_DEV = 1
RADIAL = 128
AX_DEV = 128
SLOTS = 256
NTH = 8
NX = 512
NBINS = 256
CELLS = 16384
N_AZ = 8
N_RX = 4


def draw_fwh_count(key, part):
    counts = jax.random.randint(jax.random.fold_in(key, 11), (N_AZ * N_RX,), 1, SLOTS + 1, dtype=jnp.int32)
    chosen = jax.random.randint(jax.random.fold_in(key, 12), (), 0, N_AZ * N_RX, dtype=jnp.int32)
    counts = counts.at[chosen].set(SLOTS)
    return counts.reshape(N_AZ, N_RX)


def plant(result, key, smallest, high):
    extent = result.shape
    index_at = [jax.random.randint(jax.random.fold_in(key, axis), (), 0, extent[axis]) for axis in range(len(extent))]
    result = result.at[tuple(index_at)].set(smallest)
    longest = extent.index(max(extent))
    index_at[longest] = (index_at[longest] + 1) % extent[longest]
    return result.at[tuple(index_at)].set(high)


def levels(rng, shape, cuts, smallest, largest):
    loudness, own = 1.0, jax.random.fold_in(rng, 6)
    for axis_at, shards_of in cuts:
        heights = jnp.exp(jax.random.uniform(jax.random.fold_in(own, axis_at), (shards_of,), jnp.float32, smallest / len(cuts), largest / len(cuts)))
        loudness = loudness * jnp.repeat(heights, shape[axis_at] // shards_of).reshape([-1 if axis == axis_at else 1 for axis in range(len(shape))])
    return loudness


def scatter_about(own_key, dims, spread, limit, shards=(), held_as=jnp.bfloat16):
    entries = jax.random.normal(own_key, dims, jnp.float32) * spread
    if len(shards) > 0:
        entries = levels(own_key, dims, shards, -0.22, 0.18) * entries
    return jnp.clip(entries, min=-limit, max=limit).astype(held_as)


def setup_inputs(seed: int = 0) -> dict:
    splits = jax.random.split(jax.random.key(seed), 9)
    return {
        "adjoint": scatter_about(splits[0], (5, NTH, RADIAL, NX), 1.0, 6.0, ((1, 8), (3, 4)), jnp.float32),
        "density": jnp.clip(0.6 + 0.79999995 * jax.random.uniform(splits[1], (NTH, RADIAL, NX), jnp.float32) ** levels(splits[1], (NTH, RADIAL, NX), ((0, 8), (2, 4)), -0.2, 0.2), 0.6, 1.4),
        "velocity": jnp.clip(jax.random.uniform(splits[2], (3, NTH, RADIAL, NX), jnp.float32, -0.9, 0.9) * levels(splits[2], (3, NTH, RADIAL, NX), ((1, 8), (3, 4)), -0.4, 0.0), -0.9, 0.9),
        "pressure": jnp.clip(0.5 + 0.39999998 * jax.random.uniform(splits[3], (NTH, RADIAL, NX), jnp.float32) ** levels(splits[3], (NTH, RADIAL, NX), ((0, 8), (2, 4)), -0.2, 0.2), 0.5, 0.9),
        "fwh_cell": plant(jax.random.randint(splits[4], (N_AZ, N_RX, SLOTS), 0, CELLS), jax.random.fold_in(splits[4], 1), 0, CELLS - 1).astype(jnp.int32),
        "fwh_bin": plant(jax.random.randint(splits[5], (N_AZ, N_RX, SLOTS), 0, NBINS), jax.random.fold_in(splits[5], 1), 0, NBINS - 1).astype(jnp.int32),
        "fwh_weight": scatter_about(splits[6], (N_AZ, N_RX, SLOTS), 1.0, 6.0, ((0, 8), (1, 4)), jnp.float32),
        "fwh_count": draw_fwh_count(jax.random.fold_in(splits[8], 71), 0),
    }


ALPHA_FILTER = 0.495
COEF_ZERO = 11.0 / 16.0 + 5.0 * ALPHA_FILTER / 8.0
COEF_ONE = 15.0 / 32.0 + 17.0 * ALPHA_FILTER / 16.0
COEF_TWO = -3.0 / 16.0 + 3.0 * ALPHA_FILTER / 8.0
COEF_THREE = 1.0 / 32.0 - ALPHA_FILTER / 16.0
ALPHA_DERIV = 1.0 / 3.0
NEAR_COEF = 14.0 / 9.0
FAR_COEF = 1.0 / 9.0
AXIAL_STEP = 0.02
RADIAL_STEP = 0.02
INNER_RADIUS = 0.3
SECTION_STEP = 0.004
GAMMA_GAS = 1.4


def mode_gains(count):
    angle = jnp.arange(count, dtype=jnp.int32).astype(jnp.float32) * (2.0 * math.pi / count)
    cosine = jnp.cos(angle)
    filter_gain = (COEF_ZERO + COEF_ONE * cosine + COEF_TWO * jnp.cos(2.0 * angle) + COEF_THREE * jnp.cos(3.0 * angle)) / (1.0 + 2.0 * ALPHA_FILTER * cosine)
    spacing = 2.0 * math.pi / count
    deriv_gain = filter_gain * (NEAR_COEF * jnp.sin(angle) + 0.5 * FAR_COEF * jnp.sin(2.0 * angle)) / (spacing * (1.0 + 2.0 * ALPHA_DERIV * cosine))
    return filter_gain, deriv_gain


def central(padded, axis, width, step):
    def piece_at(start):
        return lax.slice_in_dim(padded, start, start + width, axis=axis)
    return (45.0 * (piece_at(4) - piece_at(2)) - 9.0 * (piece_at(5) - piece_at(1)) + (piece_at(6) - piece_at(0))) / (60.0 * step)


def adjoint_flux(grad_axial, grad_radial, grad_theta, density, velocity, pressure):
    axial_vel, radial_vel, swirl_vel = velocity[0], velocity[1], velocity[2]
    stiff = GAMMA_GAS * pressure
    inverse = 1.0 / density
    mass_term = axial_vel * grad_axial[0] + radial_vel * grad_radial[0] + swirl_vel * grad_theta[0]
    axial_term = density * grad_axial[0] + axial_vel * grad_axial[1] + stiff * grad_axial[4] + radial_vel * grad_radial[1] + swirl_vel * grad_theta[1]
    radial_term = axial_vel * grad_axial[2] + density * grad_radial[0] + radial_vel * grad_radial[2] + stiff * grad_radial[4] + swirl_vel * grad_theta[2]
    swirl_term = axial_vel * grad_axial[3] + radial_vel * grad_radial[3] + density * grad_theta[0] + swirl_vel * grad_theta[3] + stiff * grad_theta[4]
    energy_term = inverse * grad_axial[1] + axial_vel * grad_axial[4] + inverse * grad_radial[2] + radial_vel * grad_radial[4] + inverse * grad_theta[3] + swirl_vel * grad_theta[4]
    return jnp.stack([mass_term, axial_term, radial_term, swirl_term, energy_term])


def reference(adjoint, density, velocity, pressure, fwh_cell, fwh_bin, fwh_weight, fwh_count):
    filter_gain, deriv_gain = mode_gains(NTH)
    spectrum = jnp.fft.fft(adjoint, axis=1)
    filtered = jnp.real(jnp.fft.ifft(spectrum * filter_gain[None, :, None, None], axis=1)).astype(jnp.float32)
    dtheta = jnp.real(jnp.fft.ifft(spectrum * (1j * deriv_gain)[None, :, None, None], axis=1)).astype(jnp.float32)
    pad_axial = jnp.pad(filtered, ((0, 0), (0, 0), (0, 0), (3, 3)))
    daxial = central(pad_axial, 3, NX, AXIAL_STEP)
    pad_radial = jnp.pad(filtered, ((0, 0), (0, 0), (3, 3), (0, 0)))
    dradial = central(pad_radial, 2, RADIAL, RADIAL_STEP)
    radius = (INNER_RADIUS + (jnp.arange(RADIAL, dtype=jnp.int32).astype(jnp.float32) + 0.5) * RADIAL_STEP).reshape(RADIAL, 1)
    flux = adjoint_flux(daxial, dradial, dtheta / radius, density, velocity, pressure)
    section = filtered + SECTION_STEP * flux
    blocks = section.reshape(5, N_AZ, AZ_DEV, RADIAL, N_RX, AX_DEV).transpose(1, 4, 0, 2, 3, 5).reshape(N_AZ, N_RX, 5, CELLS)
    picked = jnp.take_along_axis(blocks, fwh_cell[:, :, None, :].astype(jnp.int32), axis=3)
    live = jnp.arange(SLOTS, dtype=jnp.int32)[None, None, :] < fwh_count[:, :, None]
    values = jnp.where(live, fwh_weight * (picked[:, :, 4] + picked[:, :, 1]), 0.0)
    signal = jax.ops.segment_sum(values.reshape(-1), fwh_bin.reshape(-1), num_segments=NBINS)
    return section, signal
```

```python
import functools
import math

import jax
import jax.numpy as jnp
import numpy as np
from jax import lax
from jax.experimental import pallas as pl
from jax.experimental.pallas import tpu as pltpu
from jax.sharding import PartitionSpec as P

BIN_DEV = 8
LANES = 128
SUB = 4
EDGE = 3
SLOT = 16

ALPHA_FILTER = 0.495
COEF_ZERO = 11.0 / 16.0 + 5.0 * ALPHA_FILTER / 8.0
COEF_ONE = 15.0 / 32.0 + 17.0 * ALPHA_FILTER / 16.0
COEF_TWO = -3.0 / 16.0 + 3.0 * ALPHA_FILTER / 8.0
COEF_THREE = 1.0 / 32.0 - ALPHA_FILTER / 16.0
ALPHA_DERIV = 1.0 / 3.0
NEAR_COEF = 14.0 / 9.0
FAR_COEF = 1.0 / 9.0
AXIAL_STEP = 0.02
RADIAL_STEP = 0.02
INNER_RADIUS = 0.3
SECTION_STEP = 0.004
GAMMA_GAS = 1.4
HIGHEST = lax.Precision.HIGHEST


def kernel_values(count):
    modes = np.arange(count)
    angle = modes * (2.0 * math.pi / count)
    cosine = np.cos(angle)
    filter_gain = (
        COEF_ZERO
        + COEF_ONE * cosine
        + COEF_TWO * np.cos(2.0 * angle)
        + COEF_THREE * np.cos(3.0 * angle)
    ) / (1.0 + 2.0 * ALPHA_FILTER * cosine)
    spacing = 2.0 * math.pi / count
    deriv_gain = (
        filter_gain
        * (NEAR_COEF * np.sin(angle) + 0.5 * FAR_COEF * np.sin(2.0 * angle))
        / (spacing * (1.0 + 2.0 * ALPHA_DERIV * cosine))
    )
    phase = np.mod(modes[:, None] * modes[None, :], count) * (2.0 * math.pi / count)
    smooth = np.sum(filter_gain * np.cos(phase), axis=-1) / count
    slope = -np.sum(deriv_gain * np.sin(phase), axis=-1) / count
    return smooth, slope


def dot_up(weights, values):
    total = None
    for weight, value in zip(weights, values, strict=True):
        term = np.float32(weight) * value
        total = term if total is None else total + term
    return total


def convolve(kernel, sums, diffs):
    half = len(sums)
    first, second = [], []
    for i in range(half):
        near = [kernel[(i - j) % (2 * half)] for j in range(half)]
        far = [kernel[(i - j + half) % (2 * half)] for j in range(half)]
        even = dot_up([0.5 * (n + f) for n, f in zip(near, far)], sums)
        odd = dot_up([0.5 * (n - f) for n, f in zip(near, far)], diffs)
        first.append(even + odd)
        second.append(even - odd)
    return first + second


def pack_body(blocks, source, target):
    fields, radial = source.shape[0], source.shape[2]
    for field in range(fields):
        for row in range(0, radial, 2 * SUB):
            tile = source[field, 0, pl.ds(row, 2 * SUB), :]
            at = (field * radial + row) // SUB
            for part in range(2):
                target[(at + part) // blocks, (at + part) % blocks] = tile[
                    part * SUB : (part + 1) * SUB
                ]


def filter_body(thetas, width, blocks, smooth, slope, source, target):
    half = thetas // 2

    for b in range(width):

        @pl.loop(0, blocks)
        def _(j, b=b):
            values = [source[t * width + b, j] for t in range(thetas)]
            sums = [values[t] + values[t + half] for t in range(half)]
            diffs = [values[t] - values[t + half] for t in range(half)]
            for t, value in enumerate(convolve(smooth, sums, diffs)):
                target[t * width + b, j] = value
            for t, value in enumerate(convolve(slope, sums, diffs)):
                target[t * width + b, blocks + j] = value

    lane = lax.broadcasted_iota(jnp.int32, (SUB, LANES), 1)
    right_side = lane < EDGE
    for t in range(thetas):
        for b in range(width):
            packed = jnp.zeros((SUB, LANES), jnp.float32)
            before, after = b - 1, b + 1
            if width == 1:
                before, after = b, b
            for j in range(blocks):
                zero = jnp.zeros((SUB, LANES), jnp.float32)
                left = target[t * width + before, j] if before >= 0 else zero
                right = target[t * width + after, j] if after < width else zero
                edges = jnp.where(right_side, right, left)
                edges = pltpu.roll(edges, SLOT * j + EDGE, 1)
                mine = (lane >= SLOT * j) & (lane < SLOT * j + 2 * EDGE)
                packed = jnp.where(mine, edges, packed)
            target[t * width + b, 2 * blocks] = packed


def final_body(
    blocks,
    devices,
    pieces,
    density,
    velocity,
    pressure,
    cells,
    bins,
    weights,
    live_count,
    section,
    totals,
    filtered,
    slopes,
    halos,
    picked,
):
    fields, radial = section.shape[0], section.shape[2]
    tile = 2 * SUB
    per_field = radial // SUB
    pad = jnp.zeros((tile, LANES), jnp.float32)
    for field in range(fields):
        filtered[field, pl.ds(0, tile), :] = pad
        filtered[field, pl.ds(tile + radial, tile), :] = pad
    for at in range(fields * per_field):
        field, row = at // per_field, SUB * (at % per_field)
        piece, j = at // blocks, at % blocks
        filtered[field, pl.ds(tile + row, SUB), :] = pieces[piece, j]
        slopes[field, pl.ds(row, SUB), :] = pieces[piece, blocks + j]
        edges = pltpu.roll(pieces[piece, 2 * blocks], LANES - (SLOT * j + EDGE), 1)
        halos[field, pl.ds(row, SUB), :] = edges

    lane = lax.broadcasted_iota(jnp.int32, (tile, LANES), 1)
    sub = lax.broadcasted_iota(jnp.int32, (tile, LANES), 0)
    unit = SECTION_STEP / (60.0 * AXIAL_STEP)
    axial = [np.float32(c * unit) for c in (45.0, -9.0, 1.0)]
    unit = SECTION_STEP / (60.0 * RADIAL_STEP)
    radially = [np.float32(c * unit) for c in (45.0, -9.0, 1.0)]

    for row in range(0, radial, tile):
        rows = pl.ds(row, tile)
        middle, g, e, s = [], [], [], []
        cell_radius = INNER_RADIUS + ((sub + row).astype(jnp.float32) + 0.5) * RADIAL_STEP
        stretch = SECTION_STEP / cell_radius
        for field in range(fields):
            here = filtered[field, pl.ds(tile + row, tile), :]
            edge = halos[field, rows, :]
            total = None
            for k in range(1, EDGE + 1):
                ahead = pltpu.roll(jnp.where(lane < k, edge, here), LANES - k, 1)
                behind = pltpu.roll(jnp.where(lane >= LANES - k, edge, here), k, 1)
                term = axial[k - 1] * (ahead - behind)
                total = term if total is None else total + term
            g.append(total)
            total = None
            for k in range(1, EDGE + 1):
                above = filtered[field, pl.ds(tile + row + k, tile), :]
                below = filtered[field, pl.ds(tile + row - k, tile), :]
                term = radially[k - 1] * (above - below)
                total = term if total is None else total + term
            e.append(total)
            s.append(slopes[field, rows, :] * stretch)
            middle.append(here)
        rho = density[0, rows, :]
        u, v, w = (velocity[i, 0, rows, :] for i in range(3))
        stiff = GAMMA_GAS * pressure[0, rows, :]
        inverse = 1.0 / rho
        moved = [u * g[i] + v * e[i] + w * s[i] for i in range(fields)]
        out = [
            middle[0] + moved[0],
            middle[1] + (moved[1] + rho * g[0] + stiff * g[4]),
            middle[2] + (moved[2] + rho * e[0] + stiff * e[4]),
            middle[3] + (moved[3] + rho * s[0] + stiff * s[4]),
            middle[4] + (moved[4] + inverse * (g[1] + e[2] + s[3])),
        ]
        for field in range(fields):
            section[field, 0, rows, :] = out[field]
        picked[rows, :] = out[4] + out[1]

    slots = cells.shape[2]
    cell = cells[0]
    shift = LANES.bit_length() - 1
    column = lax.broadcasted_iota(jnp.int32, (LANES, slots), 0)
    chosen = jnp.where(column == (cell & (LANES - 1)), 1.0, 0.0)
    lines = jnp.dot(picked[...], chosen, precision=HIGHEST, preferred_element_type=jnp.float32)
    line = lax.broadcasted_iota(jnp.int32, (radial, slots), 0)
    lines = jnp.where(line == lax.shift_right_logical(cell, shift), lines, 0.0)
    values = weights[0] * jnp.sum(lines, axis=0, keepdims=True)
    order = lax.broadcasted_iota(jnp.int32, (1, slots), 1)
    values = jnp.where(order < live_count[0, 0], values, 0.0)
    own_bin = bins[0]
    owner = lax.broadcasted_iota(jnp.int32, (devices, slots), 0)
    spread = jnp.where(owner == own_bin // BIN_DEV, values, 0.0)
    place = lax.broadcasted_iota(jnp.int32, (LANES, slots), 0)
    within = jnp.where(place == own_bin % BIN_DEV, 1.0, 0.0)
    totals[...] = lax.dot_general(
        spread,
        within,
        (((1,), (1,)), ((), ())),
        precision=HIGHEST,
        preferred_element_type=jnp.float32,
    )


def whole_block():
    return pl.BlockSpec(memory_space=pltpu.VMEM)


def local(adjoint, density, velocity, pressure, fwh_cell, fwh_bin, fwh_weight, fwh_count):
    fields, local_theta, radial, axial_cells = adjoint.shape
    thetas, blocks_x = lax.axis_size("az"), lax.axis_size("rx")
    devices = thetas * blocks_x
    assert local_theta == 1 and axial_cells == LANES
    lines = fields * radial // SUB
    everyone = lines % devices == 0
    group = ("az", "rx") if everyone else ("az",)
    members = devices if everyone else thetas
    width = members // thetas
    blocks = lines // members
    params = pltpu.CompilerParams(vmem_limit_bytes=32 * 1024 * 1024)
    f32 = jnp.float32

    pieces = pl.pallas_call(
        functools.partial(pack_body, blocks),
        out_shape=jax.ShapeDtypeStruct((members, blocks, SUB, LANES), f32),
        in_specs=[whole_block()],
        out_specs=whole_block(),
        compiler_params=params,
        name="pack",
    )(adjoint)
    pieces = lax.all_to_all(pieces, group, 0, 0, tiled=True)
    smooth, slope = kernel_values(thetas)
    pieces = pl.pallas_call(
        functools.partial(filter_body, thetas, width, blocks, smooth, slope),
        out_shape=jax.ShapeDtypeStruct((members, 2 * blocks + 1, SUB, LANES), f32),
        in_specs=[whole_block()],
        out_specs=whole_block(),
        compiler_params=params,
        name="azimuth",
    )(pieces)
    if not everyone:
        own = pieces[:, 2 * blocks]
        up = [(i, i + 1) for i in range(blocks_x - 1)]
        down = [(j, i) for i, j in up]
        before, after = lax.ppermute(own, "rx", up), lax.ppermute(own, "rx", down)
        lane = jnp.arange(LANES, dtype=jnp.int32) % SLOT
        pieces = pieces.at[:, 2 * blocks].set(jnp.where(lane < EDGE, before, after))
    pieces = lax.all_to_all(pieces, group, 0, 0, tiled=True)
    section, totals = pl.pallas_call(
        functools.partial(final_body, blocks, devices),
        out_shape=(
            jax.ShapeDtypeStruct(adjoint.shape, f32),
            jax.ShapeDtypeStruct((devices, LANES), f32),
        ),
        in_specs=[whole_block()] * 7 + [pl.BlockSpec(memory_space=pltpu.SMEM)],
        out_specs=(whole_block(), whole_block()),
        scratch_shapes=[
            pltpu.VMEM((fields, radial + 4 * SUB, LANES), f32),
            pltpu.VMEM((fields, radial, LANES), f32),
            pltpu.VMEM((fields, radial, LANES), f32),
            pltpu.VMEM((radial, LANES), f32),
        ],
        compiler_params=params,
        name="section",
    )(pieces, density, velocity, pressure, fwh_cell, fwh_bin, fwh_weight, fwh_count)
    totals = lax.all_to_all(totals, ("az", "rx"), 0, 0, tiled=True)
    return section, jnp.sum(totals, axis=0)[:BIN_DEV]


def solution(mesh):
    placed = (
        P(None, "az", None, "rx"),
        P("az", None, "rx"),
        P(None, "az", None, "rx"),
        P("az", None, "rx"),
        P("az", "rx", None),
        P("az", "rx", None),
        P("az", "rx", None),
        P("az", "rx"),
    )
    return jax.shard_map(
        local,
        mesh=mesh,
        in_specs=placed,
        out_specs=(P(None, "az", None, "rx"), P(("az", "rx"))),
        check_vma=False,
    )
```

```python
import functools
import math

import jax
import jax.numpy as jnp
import numpy as np
from jax import lax
from jax.experimental import pallas as pl
from jax.experimental.pallas import tpu as pltpu
from jax.sharding import PartitionSpec as P

BIN_DEV = 8
LANES = 128
TILE = 8
EDGE = 3
SLOT = 8

ALPHA_FILTER = 0.495
COEF_ZERO = 11.0 / 16.0 + 5.0 * ALPHA_FILTER / 8.0
COEF_ONE = 15.0 / 32.0 + 17.0 * ALPHA_FILTER / 16.0
COEF_TWO = -3.0 / 16.0 + 3.0 * ALPHA_FILTER / 8.0
COEF_THREE = 1.0 / 32.0 - ALPHA_FILTER / 16.0
ALPHA_DERIV = 1.0 / 3.0
NEAR_COEF = 14.0 / 9.0
FAR_COEF = 1.0 / 9.0
AXIAL_STEP = 0.02
RADIAL_STEP = 0.02
INNER_RADIUS = 0.3
SECTION_STEP = 0.004
GAMMA_GAS = 1.4
HIGHEST = lax.Precision.HIGHEST


def kernel_values(count):
    modes = np.arange(count)
    angle = modes * (2.0 * math.pi / count)
    cosine = np.cos(angle)
    filter_gain = (
        COEF_ZERO
        + COEF_ONE * cosine
        + COEF_TWO * np.cos(2.0 * angle)
        + COEF_THREE * np.cos(3.0 * angle)
    ) / (1.0 + 2.0 * ALPHA_FILTER * cosine)
    spacing = 2.0 * math.pi / count
    deriv_gain = (
        filter_gain
        * (NEAR_COEF * np.sin(angle) + 0.5 * FAR_COEF * np.sin(2.0 * angle))
        / (spacing * (1.0 + 2.0 * ALPHA_DERIV * cosine))
    )
    phase = np.mod(modes[:, None] * modes[None, :], count) * (2.0 * math.pi / count)
    smooth = np.sum(filter_gain * np.cos(phase), axis=-1) / count
    slope = -np.sum(deriv_gain * np.sin(phase), axis=-1) / count
    return smooth, slope


def ring_order(count):
    return list(range(0, count, 2)) + list(range(count - 1, 0, -2))


def ring_weights(count):
    order = ring_order(count)
    smooth, slope = kernel_values(count)
    rows = []
    for i in range(count):
        at = order.index(i)
        hops = [0]
        for s in range(1, count // 2):
            hops += [-s, s]
        hops.append(count // 2)
        away = [(i - order[(at + hop) % count]) % count for hop in hops]
        rows.append([smooth[d] for d in away] + [slope[d] for d in away])
    return np.array(rows, np.float32)


def packed_edges(tiles):
    lane = lax.broadcasted_iota(jnp.int32, (TILE, LANES), 1)
    packed = jnp.zeros((TILE, LANES), jnp.float32)
    for k, tile in enumerate(tiles):
        moved = pltpu.roll(tile, (SLOT * k + EDGE) % LANES, 1)
        packed = jnp.where(lax.shift_right_logical(lane, 3) == k, moved, packed)
    return packed


def edges_body(source, edges):
    fields, radial = source.shape[0], source.shape[2]
    for field in range(fields):
        tiles = [source[field, 0, pl.ds(row, TILE), :] for row in range(0, radial, TILE)]
        edges[field] = packed_edges(tiles)


def partial_body(blocks, weights, source, *refs):
    count = weights.shape[1] // 2
    halves, (smooth, slope, edges) = refs[: 2 * blocks], refs[2 * blocks :]
    fields, radial = source.shape[0], source.shape[2]
    half = halves[0].shape[0]
    for field in range(fields):
        tiles = []
        for row in range(0, radial, TILE):
            at = field * radial + row
            value = source[field, 0, pl.ds(row, TILE), :]
            first, second = weights[0, 0] * value, weights[0, count] * value
            for k in range(blocks):
                value = halves[2 * k + at // half][pl.ds(at % half, TILE), :]
                first = first + weights[0, 1 + k] * value
                second = second + weights[0, count + 1 + k] * value
            smooth[pl.ds(at, TILE), :] = first
            slope[pl.ds(at, TILE), :] = second
            tiles.append(first)
        edges[field] = packed_edges(tiles)


def final_body(
    devices,
    weights,
    live_count,
    smooth,
    slope,
    last_first,
    last_second,
    raw_before,
    raw_after,
    sum_before,
    sum_after,
    density,
    velocity,
    pressure,
    cells,
    bins,
    slot_weights,
    section,
    totals,
    filtered,
    picked,
):
    fields, radial = section.shape[0], section.shape[2]
    count = weights.shape[1] // 2
    half = last_first.shape[0]
    last_weight, last_slope = weights[0, count - 1], weights[0, 2 * count - 1]

    def last(at):
        source = last_first if at < half else last_second
        return source[pl.ds(at % half, TILE), :]

    lane = lax.broadcasted_iota(jnp.int32, (TILE, LANES), 1)
    sub = lax.broadcasted_iota(jnp.int32, (TILE, LANES), 0)
    pad = jnp.zeros((TILE, LANES), jnp.float32)
    halos = []
    for field in range(fields):
        filtered[field, pl.ds(0, TILE), :] = pad
        filtered[field, pl.ds(TILE + radial, TILE), :] = pad
        for row in range(0, radial, TILE):
            at = field * radial + row
            value = smooth[pl.ds(at, TILE), :] + last_weight * last(at)
            filtered[field, pl.ds(TILE + row, TILE), :] = value
        before = sum_before[field] + last_weight * raw_before[field]
        after = sum_after[field] + last_weight * raw_after[field]
        halos.append(jnp.where((lane & (SLOT - 1)) < EDGE, before, after))

    unit = SECTION_STEP / (60.0 * AXIAL_STEP)
    axial = [np.float32(c * unit) for c in (45.0, -9.0, 1.0)]
    unit = SECTION_STEP / (60.0 * RADIAL_STEP)
    radially = [np.float32(c * unit) for c in (45.0, -9.0, 1.0)]

    for row in range(0, radial, TILE):
        rows = pl.ds(row, TILE)
        middle, g, e, s = [], [], [], []
        cell_radius = INNER_RADIUS + ((sub + row).astype(jnp.float32) + 0.5) * RADIAL_STEP
        stretch = SECTION_STEP / cell_radius
        for field in range(fields):
            here = filtered[field, pl.ds(TILE + row, TILE), :]
            edge = pltpu.roll(halos[field], LANES - (SLOT * (row // TILE) + EDGE), 1)
            total = None
            for k in range(1, EDGE + 1):
                ahead = pltpu.roll(jnp.where(lane < k, edge, here), LANES - k, 1)
                behind = pltpu.roll(jnp.where(lane >= LANES - k, edge, here), k, 1)
                term = axial[k - 1] * (ahead - behind)
                total = term if total is None else total + term
            g.append(total)
            total = None
            for k in range(1, EDGE + 1):
                above = filtered[field, pl.ds(TILE + row + k, TILE), :]
                below = filtered[field, pl.ds(TILE + row - k, TILE), :]
                term = radially[k - 1] * (above - below)
                total = term if total is None else total + term
            e.append(total)
            at = field * radial + row
            s.append((slope[pl.ds(at, TILE), :] + last_slope * last(at)) * stretch)
            middle.append(here)
        rho = density[0, rows, :]
        u, v, w = (velocity[i, 0, rows, :] for i in range(3))
        stiff = GAMMA_GAS * pressure[0, rows, :]
        inverse = 1.0 / rho
        moved = [u * g[i] + v * e[i] + w * s[i] for i in range(fields)]
        out = [
            middle[0] + moved[0],
            middle[1] + (moved[1] + rho * g[0] + stiff * g[4]),
            middle[2] + (moved[2] + rho * e[0] + stiff * e[4]),
            middle[3] + (moved[3] + rho * s[0] + stiff * s[4]),
            middle[4] + (moved[4] + inverse * (g[1] + e[2] + s[3])),
        ]
        for field in range(fields):
            section[field, 0, rows, :] = out[field]
        picked[rows, :] = out[4] + out[1]

    slots = cells.shape[2]
    cell = cells[0]
    shift = LANES.bit_length() - 1
    column = lax.broadcasted_iota(jnp.int32, (LANES, slots), 0)
    chosen = jnp.where(column == (cell & (LANES - 1)), 1.0, 0.0)
    lines = jnp.dot(picked[...], chosen, precision=HIGHEST, preferred_element_type=jnp.float32)
    line = lax.broadcasted_iota(jnp.int32, (radial, slots), 0)
    lines = jnp.where(line == lax.shift_right_logical(cell, shift), lines, 0.0)
    values = slot_weights[0] * jnp.sum(lines, axis=0, keepdims=True)
    order = lax.broadcasted_iota(jnp.int32, (1, slots), 1)
    values = jnp.where(order < live_count[0, 0], values, 0.0)
    own_bin = bins[0]
    owner = lax.broadcasted_iota(jnp.int32, (devices, slots), 0)
    spread = jnp.where(owner == own_bin // BIN_DEV, values, 0.0)
    place = lax.broadcasted_iota(jnp.int32, (LANES, slots), 0)
    within = jnp.where(place == own_bin % BIN_DEV, 1.0, 0.0)
    totals[...] = lax.dot_general(
        spread,
        within,
        (((1,), (1,)), ((), ())),
        precision=HIGHEST,
        preferred_element_type=jnp.float32,
    )


def in_vmem(count):
    return [pl.BlockSpec(memory_space=pltpu.VMEM)] * count


def in_smem(count):
    return [pl.BlockSpec(memory_space=pltpu.SMEM)] * count


def local(adjoint, density, velocity, pressure, fwh_cell, fwh_bin, fwh_weight, fwh_count):
    fields, local_theta, radial, axial_cells = adjoint.shape
    thetas, blocks_x = lax.axis_size("az"), lax.axis_size("rx")
    devices = thetas * blocks_x
    assert local_theta == 1 and axial_cells == LANES and thetas % 2 == 0
    assert radial % TILE == 0 and radial // TILE * SLOT <= LANES
    params = pltpu.CompilerParams(vmem_limit_bytes=40 * 1024 * 1024)
    f32 = jnp.float32
    rows = fields * radial
    half = rows // 2
    edge_shape = jax.ShapeDtypeStruct((fields, TILE, LANES), f32)

    table = jnp.asarray(ring_weights(thetas))
    weights = lax.dynamic_slice_in_dim(table, lax.axis_index("az"), 1, axis=0)

    order = ring_order(thetas)
    onward = [(order[i], order[(i + 1) % thetas]) for i in range(thetas)]
    back = [(b, a) for a, b in onward]
    across = {order[i]: order[(i + thetas // 2) % thetas] for i in range(thetas)}

    flat = adjoint.reshape(rows, LANES)
    own = [flat[:half], flat[half:]]
    edges = pl.pallas_call(
        edges_body,
        out_shape=edge_shape,
        in_specs=in_vmem(1),
        out_specs=in_vmem(1)[0],
        compiler_params=params,
        name="edges",
    )(adjoint)

    def beyond(step):
        return [
            (i * blocks_x + b, across[i] * blocks_x + b + step)
            for i in range(thetas)
            for b in range(blocks_x)
            if 0 <= b + step < blocks_x
        ]

    from_left, from_right, halves = list(own), list(own), []
    raw_before = raw_after = None
    for step in range(1, thetas // 2):
        left, right = [], []
        for part in range(2):
            left.append(lax.ppermute(from_left[part], "az", onward))
            right.append(lax.ppermute(from_right[part], "az", back))
        from_left, from_right = left, right
        halves += left + right
        if step == 1:
            raw_before = lax.ppermute(edges, ("az", "rx"), beyond(1))
            raw_after = lax.ppermute(edges, ("az", "rx"), beyond(-1))
    last_first = lax.ppermute(from_left[0], "az", onward)
    last_second = lax.ppermute(from_right[1], "az", back)

    blocks = len(halves) // 2
    smooth, slope, sums = pl.pallas_call(
        functools.partial(partial_body, blocks),
        out_shape=(
            jax.ShapeDtypeStruct((rows, LANES), f32),
            jax.ShapeDtypeStruct((rows, LANES), f32),
            edge_shape,
        ),
        in_specs=in_smem(1) + in_vmem(1 + 2 * blocks),
        out_specs=tuple(in_vmem(3)),
        compiler_params=params,
        name="partial",
    )(weights, adjoint, *halves)
    up = [(i, i + 1) for i in range(blocks_x - 1)]
    down = [(j, i) for i, j in up]
    sum_before, sum_after = lax.ppermute(sums, "rx", up), lax.ppermute(sums, "rx", down)

    section, totals = pl.pallas_call(
        functools.partial(final_body, devices),
        out_shape=(
            jax.ShapeDtypeStruct(adjoint.shape, f32),
            jax.ShapeDtypeStruct((devices, LANES), f32),
        ),
        in_specs=in_smem(2) + in_vmem(14),
        out_specs=tuple(in_vmem(2)),
        scratch_shapes=[
            pltpu.VMEM((fields, radial + 2 * TILE, LANES), f32),
            pltpu.VMEM((radial, LANES), f32),
        ],
        compiler_params=params,
        name="section",
    )(
        weights,
        fwh_count,
        smooth,
        slope,
        last_first,
        last_second,
        raw_before,
        raw_after,
        sum_before,
        sum_after,
        density,
        velocity,
        pressure,
        fwh_cell,
        fwh_bin,
        fwh_weight,
    )
    totals = lax.all_to_all(totals, ("az", "rx"), 0, 0, tiled=True)
    return section, jnp.sum(totals, axis=0)[:BIN_DEV]


def solution(mesh):
    placed = (
        P(None, "az", None, "rx"),
        P("az", None, "rx"),
        P(None, "az", None, "rx"),
        P("az", None, "rx"),
        P("az", "rx", None),
        P("az", "rx", None),
        P("az", "rx", None),
        P("az", "rx"),
    )
    return jax.shard_map(
        local,
        mesh=mesh,
        in_specs=placed,
        out_specs=(P(None, "az", None, "rx"), P(("az", "rx"))),
        check_vma=False,
    )
```

```python
import functools
import math

import jax
import jax.numpy as jnp
import numpy as np
from jax import lax
from jax.experimental import pallas as pl
from jax.experimental.pallas import tpu as pltpu
from jax.sharding import PartitionSpec as P

BIN_DEV = 8
LANES = 128
TILE = 8
EDGE = 3
SLOT = 8

ALPHA_FILTER = 0.495
COEF_ZERO = 11.0 / 16.0 + 5.0 * ALPHA_FILTER / 8.0
COEF_ONE = 15.0 / 32.0 + 17.0 * ALPHA_FILTER / 16.0
COEF_TWO = -3.0 / 16.0 + 3.0 * ALPHA_FILTER / 8.0
COEF_THREE = 1.0 / 32.0 - ALPHA_FILTER / 16.0
ALPHA_DERIV = 1.0 / 3.0
NEAR_COEF = 14.0 / 9.0
FAR_COEF = 1.0 / 9.0
AXIAL_STEP = 0.02
RADIAL_STEP = 0.02
INNER_RADIUS = 0.3
SECTION_STEP = 0.004
GAMMA_GAS = 1.4


def kernel_values(count):
    modes = np.arange(count)
    angle = modes * (2.0 * math.pi / count)
    cosine = np.cos(angle)
    filter_gain = (
        COEF_ZERO
        + COEF_ONE * cosine
        + COEF_TWO * np.cos(2.0 * angle)
        + COEF_THREE * np.cos(3.0 * angle)
    ) / (1.0 + 2.0 * ALPHA_FILTER * cosine)
    spacing = 2.0 * math.pi / count
    deriv_gain = (
        filter_gain
        * (NEAR_COEF * np.sin(angle) + 0.5 * FAR_COEF * np.sin(2.0 * angle))
        / (spacing * (1.0 + 2.0 * ALPHA_DERIV * cosine))
    )
    phase = np.mod(modes[:, None] * modes[None, :], count) * (2.0 * math.pi / count)
    smooth = np.sum(filter_gain * np.cos(phase), axis=-1) / count
    slope = -np.sum(deriv_gain * np.sin(phase), axis=-1) / count
    return smooth, slope


def ring_order(count):
    return list(range(0, count, 2)) + list(range(count - 1, 0, -2))


def ring_weights(count):
    order = ring_order(count)
    smooth, slope = kernel_values(count)
    rows = []
    for i in range(count):
        at = order.index(i)
        hops = [0]
        for s in range(1, count // 2):
            hops += [-s, s]
        hops.append(count // 2)
        away = [(i - order[(at + hop) % count]) % count for hop in hops]
        rows.append([smooth[d] for d in away] + [slope[d] for d in away])
    return np.array(rows, np.float32)


def packed_edges(tiles):
    lane = lax.broadcasted_iota(jnp.int32, (TILE, LANES), 1)
    packed = jnp.zeros((TILE, LANES), jnp.float32)
    for k, tile in enumerate(tiles):
        moved = pltpu.roll(tile, (SLOT * k + EDGE) % LANES, 1)
        packed = jnp.where(lax.shift_right_logical(lane, 3) == k, moved, packed)
    return packed


def partial_body(blocks, weights, source, *refs):
    count = weights.shape[1] // 2
    halves, (smooth, slope) = refs[: 2 * blocks], refs[2 * blocks :]
    fields, radial = source.shape[0], source.shape[2]
    half = halves[0].shape[0]
    for field in range(fields):
        for row in range(0, radial, TILE):
            at = field * radial + row
            value = source[field, 0, pl.ds(row, TILE), :]
            first, second = weights[0, 0] * value, weights[0, count] * value
            for k in range(blocks):
                value = halves[2 * k + at // half][pl.ds(at % half, TILE), :]
                first = first + weights[0, 1 + k] * value
                second = second + weights[0, count + 1 + k] * value
            smooth[pl.ds(at, TILE), :] = first
            slope[pl.ds(at, TILE), :] = second


def finish_body(weights, smooth, last_first, last_second, filtered, edges):
    fields, count = edges.shape[0], weights.shape[1] // 2
    half = last_first.shape[0]
    radial = smooth.shape[0] // fields
    last_weight = weights[0, count - 1]
    for field in range(fields):
        tiles = []
        for row in range(0, radial, TILE):
            at = field * radial + row
            source = last_first if at < half else last_second
            value = smooth[pl.ds(at, TILE), :] + last_weight * source[pl.ds(at % half, TILE), :]
            filtered[pl.ds(at, TILE), :] = value
            tiles.append(value)
        edges[field] = packed_edges(tiles)


def slots_body(live_count, cells, bins, slot_weights, column, line, owner, place):
    slots = cells.shape[2]
    cell, own_bin = cells[0], bins[0]
    order = lax.broadcasted_iota(jnp.int32, (1, slots), 1)
    weight = jnp.where(order < live_count[0, 0], slot_weights[0], 0.0)

    def table(target, index, value):
        rows = lax.broadcasted_iota(jnp.int32, target.shape, 0)
        target[...] = jnp.where(rows == index, value, 0.0).astype(target.dtype)

    table(column, cell & (LANES - 1), 1.0)
    table(line, lax.shift_right_logical(cell, LANES.bit_length() - 1), weight)
    table(owner, own_bin // BIN_DEV, 1.0)
    table(place, own_bin % BIN_DEV, 1.0)


def three_parts(value):
    parts = []
    for _ in range(3):
        part = value.astype(jnp.bfloat16)
        parts.append(part)
        value = value - part.astype(jnp.float32)
    return jnp.concatenate(parts, axis=0)


def add_parts(stacked):
    rows = stacked.shape[0] // 3
    return stacked[:rows] + (stacked[rows : 2 * rows] + stacked[2 * rows :])


def final_body(
    blocks_x,
    weights,
    place_x,
    smooth,
    slope,
    last_first,
    last_second,
    edges_pair,
    edges_next,
    density,
    velocity,
    pressure,
    column,
    line,
    owner,
    place,
    section,
    totals,
    filtered,
    halos,
    picked,
):
    fields, radial = section.shape[0], section.shape[2]
    count = weights.shape[1] // 2
    half = last_first.shape[0]
    last_slope = weights[0, 2 * count - 1]

    def last(at):
        source = last_first if at < half else last_second
        return source[pl.ds(at % half, TILE), :]

    lane = lax.broadcasted_iota(jnp.int32, (TILE, LANES), 1)
    sub = lax.broadcasted_iota(jnp.int32, (TILE, LANES), 0)
    odd = (place_x[0, 0] & 1) == 1
    paired = ((lane & (SLOT - 1)) < EDGE) == odd
    inner = jnp.where((place_x[0, 0] == 0) | (place_x[0, 0] == blocks_x - 1), 0.0, 1.0)
    pad = jnp.zeros((TILE, LANES), jnp.float32)
    for field in range(fields):
        filtered[field, pl.ds(0, TILE), :] = pad
        filtered[field, pl.ds(TILE + radial, TILE), :] = pad
        packed = jnp.where(paired, edges_pair[field], inner * edges_next[field])
        for row in range(0, radial, TILE):
            at = field * radial + row
            filtered[field, pl.ds(TILE + row, TILE), :] = smooth[pl.ds(at, TILE), :]
            edge = pltpu.roll(packed, LANES - (SLOT * (row // TILE) + EDGE), 1)
            halos[field, pl.ds(row, TILE), :] = edge

    unit = SECTION_STEP / (60.0 * AXIAL_STEP)
    axial = [np.float32(c * unit) for c in (45.0, -9.0, 1.0)]
    unit = SECTION_STEP / (60.0 * RADIAL_STEP)
    radially = [np.float32(c * unit) for c in (45.0, -9.0, 1.0)]

    for row in range(0, radial, TILE):
        rows = pl.ds(row, TILE)
        middle, g, e, s = [], [], [], []
        cell_radius = INNER_RADIUS + ((sub + row).astype(jnp.float32) + 0.5) * RADIAL_STEP
        stretch = SECTION_STEP / cell_radius
        for field in range(fields):
            here = filtered[field, pl.ds(TILE + row, TILE), :]
            edge = halos[field, rows, :]
            total = None
            for k in range(1, EDGE + 1):
                ahead = pltpu.roll(jnp.where(lane < k, edge, here), LANES - k, 1)
                behind = pltpu.roll(jnp.where(lane >= LANES - k, edge, here), k, 1)
                term = axial[k - 1] * (ahead - behind)
                total = term if total is None else total + term
            g.append(total)
            total = None
            for k in range(1, EDGE + 1):
                above = filtered[field, pl.ds(TILE + row + k, TILE), :]
                below = filtered[field, pl.ds(TILE + row - k, TILE), :]
                term = radially[k - 1] * (above - below)
                total = term if total is None else total + term
            e.append(total)
            at = field * radial + row
            s.append((slope[pl.ds(at, TILE), :] + last_slope * last(at)) * stretch)
            middle.append(here)
        rho = density[0, rows, :]
        u, v, w = (velocity[i, 0, rows, :] for i in range(3))
        stiff = GAMMA_GAS * pressure[0, rows, :]
        inverse = 1.0 / rho
        moved = [u * g[i] + v * e[i] + w * s[i] for i in range(fields)]
        out = [
            middle[0] + moved[0],
            middle[1] + (moved[1] + rho * g[0] + stiff * g[4]),
            middle[2] + (moved[2] + rho * e[0] + stiff * e[4]),
            middle[3] + (moved[3] + rho * s[0] + stiff * s[4]),
            middle[4] + (moved[4] + inverse * (g[1] + e[2] + s[3])),
        ]
        for field in range(fields):
            section[field, 0, rows, :] = out[field]
        picked[rows, :] = out[4] + out[1]

    lines = jnp.dot(three_parts(picked[...]), column[...], preferred_element_type=jnp.float32)
    values = jnp.sum(line[...] * add_parts(lines), axis=0, keepdims=True)
    spread = three_parts(owner[...] * values)
    totals[...] = add_parts(
        lax.dot_general(
            spread, place[...], (((1,), (1,)), ((), ())), preferred_element_type=jnp.float32
        )
    )


def store_body(source, target, semaphore):
    copy = pltpu.make_async_copy(source, target, semaphore)
    copy.start()
    copy.wait()


def in_vmem(count):
    return [pl.BlockSpec(memory_space=pltpu.VMEM)] * count


def in_smem(count):
    return [pl.BlockSpec(memory_space=pltpu.SMEM)] * count


def local(adjoint, density, velocity, pressure, fwh_cell, fwh_bin, fwh_weight, fwh_count):
    fields, local_theta, radial, axial_cells = adjoint.shape
    thetas, blocks_x = lax.axis_size("az"), lax.axis_size("rx")
    devices = thetas * blocks_x
    assert local_theta == 1 and axial_cells == LANES and thetas % 2 == 0 and blocks_x % 2 == 0
    assert radial % TILE == 0 and radial // TILE * SLOT <= LANES
    params = pltpu.CompilerParams(vmem_limit_bytes=40 * 1024 * 1024)
    f32 = jnp.float32
    rows = fields * radial
    half, slots = rows // 2, fwh_cell.shape[2]
    edge_shape = jax.ShapeDtypeStruct((fields, TILE, LANES), f32)

    order = ring_order(thetas)
    onward = [(order[i], order[(i + 1) % thetas]) for i in range(thetas)]
    back = [(b, a) for a, b in onward]

    flat = adjoint.reshape(rows, LANES)
    own = [flat[:half], flat[half:]]
    steps = thetas // 2 - 1

    from_left, from_right, halves = list(own), list(own), []
    for step in range(steps):
        left, right = [], []
        for part in range(2):
            left.append(lax.ppermute(from_left[part], "az", onward))
            right.append(lax.ppermute(from_right[part], "az", back))
        from_left, from_right = left, right
        if step == 0:
            weights = lax.dynamic_slice_in_dim(
                jnp.asarray(ring_weights(thetas)), lax.axis_index("az"), 1, axis=0
            )
            tables = pl.pallas_call(
                slots_body,
                out_shape=(
                    jax.ShapeDtypeStruct((LANES, slots), jnp.bfloat16),
                    jax.ShapeDtypeStruct((radial, slots), f32),
                    jax.ShapeDtypeStruct((devices, slots), f32),
                    jax.ShapeDtypeStruct((LANES, slots), jnp.bfloat16),
                ),
                in_specs=in_smem(1) + in_vmem(3),
                out_specs=tuple(in_vmem(4)),
                compiler_params=params,
                name="slots",
            )(fwh_count, fwh_cell, fwh_bin, fwh_weight)
        if step == 1:
            weights, tables, from_right[1] = lax.optimization_barrier(
                (weights, tables, from_right[1])
            )
        halves += from_left + from_right
    last_first = lax.ppermute(from_left[0], "az", onward)
    last_second = lax.ppermute(from_right[1], "az", back)

    blocks = len(halves) // 2
    smooth, slope = pl.pallas_call(
        functools.partial(partial_body, blocks),
        out_shape=(
            jax.ShapeDtypeStruct((rows, LANES), f32),
            jax.ShapeDtypeStruct((rows, LANES), f32),
        ),
        in_specs=in_smem(1) + in_vmem(1 + 2 * blocks),
        out_specs=tuple(in_vmem(2)),
        compiler_params=params,
        name="partial",
    )(weights, adjoint, *halves)
    filtered, edges = pl.pallas_call(
        finish_body,
        out_shape=(jax.ShapeDtypeStruct((rows, LANES), f32), edge_shape),
        in_specs=in_smem(1) + in_vmem(3),
        out_specs=tuple(in_vmem(2)),
        compiler_params=params,
        name="finish",
    )(weights, smooth, last_first, last_second)
    pairs = [(b, b ^ 1) for b in range(blocks_x)]
    nexts = [(b, (b + (1 if b % 2 else -1)) % blocks_x) for b in range(blocks_x)]
    edges_next, edges_pair = lax.ppermute(edges, "rx", nexts), lax.ppermute(edges, "rx", pairs)
    place_x = jnp.reshape(lax.axis_index("rx"), (1, 1))

    held, totals = pl.pallas_call(
        functools.partial(final_body, blocks_x),
        out_shape=(
            jax.ShapeDtypeStruct(adjoint.shape, f32),
            jax.ShapeDtypeStruct((devices, LANES), f32),
        ),
        in_specs=in_smem(2) + in_vmem(13),
        out_specs=tuple(in_vmem(2)),
        scratch_shapes=[
            pltpu.VMEM((fields, radial + 2 * TILE, LANES), f32),
            pltpu.VMEM((fields, radial, LANES), f32),
            pltpu.VMEM((radial, LANES), f32),
        ],
        compiler_params=params,
        name="section",
    )(
        weights,
        place_x,
        filtered,
        slope,
        last_first,
        last_second,
        edges_pair,
        edges_next,
        density,
        velocity,
        pressure,
        *tables,
    )
    totals = lax.all_to_all(totals, ("az", "rx"), 0, 0, tiled=True)
    section = pl.pallas_call(
        store_body,
        out_shape=jax.ShapeDtypeStruct(adjoint.shape, f32),
        in_specs=[pl.BlockSpec(memory_space=pl.ANY)],
        out_specs=pl.BlockSpec(memory_space=pl.ANY),
        scratch_shapes=[pltpu.SemaphoreType.DMA],
        compiler_params=params,
        name="store",
    )(held)
    return section, jnp.sum(totals, axis=0)[:BIN_DEV]


def solution(mesh):
    placed = (
        P(None, "az", None, "rx"),
        P("az", None, "rx"),
        P(None, "az", None, "rx"),
        P("az", None, "rx"),
        P("az", "rx", None),
        P("az", "rx", None),
        P("az", "rx", None),
        P("az", "rx"),
    )
    return jax.shard_map(
        local,
        mesh=mesh,
        in_specs=placed,
        out_specs=(P(None, "az", None, "rx"), P(("az", "rx"))),
        check_vma=False,
    )
```

```python
import functools
import math

import jax
import jax.numpy as jnp
import numpy as np
from jax import lax
from jax.experimental import pallas as pl
from jax.experimental.pallas import tpu as pltpu
from jax.sharding import PartitionSpec as P

BIN_DEV = 8
LANES = 128
TILE = 8
EDGE = 3
SLOT = 8

ALPHA_FILTER = 0.495
COEF_ZERO = 11.0 / 16.0 + 5.0 * ALPHA_FILTER / 8.0
COEF_ONE = 15.0 / 32.0 + 17.0 * ALPHA_FILTER / 16.0
COEF_TWO = -3.0 / 16.0 + 3.0 * ALPHA_FILTER / 8.0
COEF_THREE = 1.0 / 32.0 - ALPHA_FILTER / 16.0
ALPHA_DERIV = 1.0 / 3.0
NEAR_COEF = 14.0 / 9.0
FAR_COEF = 1.0 / 9.0
AXIAL_STEP = 0.02
RADIAL_STEP = 0.02
INNER_RADIUS = 0.3
SECTION_STEP = 0.004
GAMMA_GAS = 1.4


def kernel_values(count):
    modes = np.arange(count)
    angle = modes * (2.0 * math.pi / count)
    cosine = np.cos(angle)
    filter_gain = (
        COEF_ZERO
        + COEF_ONE * cosine
        + COEF_TWO * np.cos(2.0 * angle)
        + COEF_THREE * np.cos(3.0 * angle)
    ) / (1.0 + 2.0 * ALPHA_FILTER * cosine)
    spacing = 2.0 * math.pi / count
    deriv_gain = (
        filter_gain
        * (NEAR_COEF * np.sin(angle) + 0.5 * FAR_COEF * np.sin(2.0 * angle))
        / (spacing * (1.0 + 2.0 * ALPHA_DERIV * cosine))
    )
    phase = np.mod(modes[:, None] * modes[None, :], count) * (2.0 * math.pi / count)
    smooth = np.sum(filter_gain * np.cos(phase), axis=-1) / count
    slope = -np.sum(deriv_gain * np.sin(phase), axis=-1) / count
    return smooth, slope


def ring_order(count):
    return list(range(0, count, 2)) + list(range(count - 1, 0, -2))


def ring_weights(count):
    order = ring_order(count)
    smooth, slope = kernel_values(count)
    rows = []
    for i in range(count):
        at = order.index(i)
        hops = [0]
        for s in range(1, count // 2):
            hops += [-s, s]
        hops.append(count // 2)
        away = [(i - order[(at + hop) % count]) % count for hop in hops]
        rows.append([smooth[d] for d in away] + [slope[d] for d in away])
    return np.array(rows, np.float32)


def packed_edges(tiles):
    lane = lax.broadcasted_iota(jnp.int32, (TILE, LANES), 1)
    packed = jnp.zeros((TILE, LANES), jnp.float32)
    for k, tile in enumerate(tiles):
        moved = pltpu.roll(tile, (SLOT * k + EDGE) % LANES, 1)
        packed = jnp.where(lax.shift_right_logical(lane, 3) == k, moved, packed)
    return packed


def edges_body(source, edges):
    fields, radial = source.shape[0], source.shape[2]
    for field in range(fields):
        tiles = [source[field, 0, pl.ds(row, TILE), :] for row in range(0, radial, TILE)]
        edges[field] = packed_edges(tiles)


def partial_body(blocks, weights, source, last_edges, *refs):
    count = weights.shape[1] // 2
    halves, (smooth, slope, edges) = refs[: 2 * blocks], refs[2 * blocks :]
    fields, radial = source.shape[0], source.shape[2]
    half = halves[0].shape[0]
    for field in range(fields):
        tiles = []
        for row in range(0, radial, TILE):
            at = field * radial + row
            value = source[field, 0, pl.ds(row, TILE), :]
            first, second = weights[0, 0] * value, weights[0, count] * value
            for k in range(blocks):
                value = halves[2 * k + at // half][pl.ds(at % half, TILE), :]
                first = first + weights[0, 1 + k] * value
                second = second + weights[0, count + 1 + k] * value
            smooth[pl.ds(at, TILE), :] = first
            slope[pl.ds(at, TILE), :] = second
            tiles.append(first)
        edges[field] = packed_edges(tiles) + weights[0, count - 1] * last_edges[field]


def slots_body(live_count, cells, bins, slot_weights, column, line, owner, place):
    slots = cells.shape[2]
    cell, own_bin = cells[0], bins[0]
    order = lax.broadcasted_iota(jnp.int32, (1, slots), 1)
    weight = jnp.where(order < live_count[0, 0], slot_weights[0], 0.0)

    def table(target, index, value):
        rows = lax.broadcasted_iota(jnp.int32, target.shape, 0)
        target[...] = jnp.where(rows == index, value, 0.0).astype(target.dtype)

    table(column, cell & (LANES - 1), 1.0)
    table(line, lax.shift_right_logical(cell, LANES.bit_length() - 1), weight)
    table(owner, own_bin // BIN_DEV, 1.0)
    table(place, own_bin % BIN_DEV, 1.0)


def three_parts(value):
    parts = []
    for _ in range(3):
        part = value.astype(jnp.bfloat16)
        parts.append(part)
        value = value - part.astype(jnp.float32)
    return jnp.concatenate(parts, axis=0)


def add_parts(stacked):
    rows = stacked.shape[0] // 3
    return stacked[:rows] + (stacked[rows : 2 * rows] + stacked[2 * rows :])


def final_body(
    blocks_x,
    weights,
    place_x,
    smooth,
    slope,
    last_first,
    last_second,
    edges_pair,
    edges_next,
    density,
    velocity,
    pressure,
    column,
    line,
    owner,
    place,
    section,
    totals,
    filtered,
    halos,
    picked,
):
    fields, radial = section.shape[0], section.shape[2]
    count = weights.shape[1] // 2
    half = last_first.shape[0]
    last_weight, last_slope = weights[0, count - 1], weights[0, 2 * count - 1]

    def last(at):
        source = last_first if at < half else last_second
        return source[pl.ds(at % half, TILE), :]

    lane = lax.broadcasted_iota(jnp.int32, (TILE, LANES), 1)
    sub = lax.broadcasted_iota(jnp.int32, (TILE, LANES), 0)
    odd = (place_x[0, 0] & 1) == 1
    paired = ((lane & (SLOT - 1)) < EDGE) == odd
    inner = jnp.where((place_x[0, 0] == 0) | (place_x[0, 0] == blocks_x - 1), 0.0, 1.0)
    pad = jnp.zeros((TILE, LANES), jnp.float32)
    for field in range(fields):
        filtered[field, pl.ds(0, TILE), :] = pad
        filtered[field, pl.ds(TILE + radial, TILE), :] = pad
        packed = jnp.where(paired, edges_pair[field], inner * edges_next[field])
        for row in range(0, radial, TILE):
            at = field * radial + row
            value = smooth[pl.ds(at, TILE), :] + last_weight * last(at)
            filtered[field, pl.ds(TILE + row, TILE), :] = value
            edge = pltpu.roll(packed, LANES - (SLOT * (row // TILE) + EDGE), 1)
            halos[field, pl.ds(row, TILE), :] = edge

    unit = SECTION_STEP / (60.0 * AXIAL_STEP)
    axial = [np.float32(c * unit) for c in (45.0, -9.0, 1.0)]
    unit = SECTION_STEP / (60.0 * RADIAL_STEP)
    radially = [np.float32(c * unit) for c in (45.0, -9.0, 1.0)]

    for row in range(0, radial, TILE):
        rows = pl.ds(row, TILE)
        middle, g, e, s = [], [], [], []
        cell_radius = INNER_RADIUS + ((sub + row).astype(jnp.float32) + 0.5) * RADIAL_STEP
        stretch = SECTION_STEP / cell_radius
        for field in range(fields):
            here = filtered[field, pl.ds(TILE + row, TILE), :]
            edge = halos[field, rows, :]
            total = None
            for k in range(1, EDGE + 1):
                ahead = pltpu.roll(jnp.where(lane < k, edge, here), LANES - k, 1)
                behind = pltpu.roll(jnp.where(lane >= LANES - k, edge, here), k, 1)
                term = axial[k - 1] * (ahead - behind)
                total = term if total is None else total + term
            g.append(total)
            total = None
            for k in range(1, EDGE + 1):
                above = filtered[field, pl.ds(TILE + row + k, TILE), :]
                below = filtered[field, pl.ds(TILE + row - k, TILE), :]
                term = radially[k - 1] * (above - below)
                total = term if total is None else total + term
            e.append(total)
            at = field * radial + row
            s.append((slope[pl.ds(at, TILE), :] + last_slope * last(at)) * stretch)
            middle.append(here)
        rho = density[0, rows, :]
        u, v, w = (velocity[i, 0, rows, :] for i in range(3))
        stiff = GAMMA_GAS * pressure[0, rows, :]
        inverse = 1.0 / rho
        moved = [u * g[i] + v * e[i] + w * s[i] for i in range(fields)]
        out = [
            middle[0] + moved[0],
            middle[1] + (moved[1] + rho * g[0] + stiff * g[4]),
            middle[2] + (moved[2] + rho * e[0] + stiff * e[4]),
            middle[3] + (moved[3] + rho * s[0] + stiff * s[4]),
            middle[4] + (moved[4] + inverse * (g[1] + e[2] + s[3])),
        ]
        for field in range(fields):
            section[field, 0, rows, :] = out[field]
        picked[rows, :] = out[4] + out[1]

    lines = jnp.dot(three_parts(picked[...]), column[...], preferred_element_type=jnp.float32)
    values = jnp.sum(line[...] * add_parts(lines), axis=0, keepdims=True)
    spread = three_parts(owner[...] * values)
    totals[...] = add_parts(
        lax.dot_general(
            spread, place[...], (((1,), (1,)), ((), ())), preferred_element_type=jnp.float32
        )
    )


def store_body(source, target, semaphore):
    copy = pltpu.make_async_copy(source, target, semaphore)
    copy.start()
    copy.wait()


def in_vmem(count):
    return [pl.BlockSpec(memory_space=pltpu.VMEM)] * count


def in_smem(count):
    return [pl.BlockSpec(memory_space=pltpu.SMEM)] * count


def local(adjoint, density, velocity, pressure, fwh_cell, fwh_bin, fwh_weight, fwh_count):
    fields, local_theta, radial, axial_cells = adjoint.shape
    thetas, blocks_x = lax.axis_size("az"), lax.axis_size("rx")
    devices = thetas * blocks_x
    assert local_theta == 1 and axial_cells == LANES and thetas % 2 == 0 and blocks_x % 2 == 0
    assert radial % TILE == 0 and radial // TILE * SLOT <= LANES
    params = pltpu.CompilerParams(vmem_limit_bytes=40 * 1024 * 1024)
    f32 = jnp.float32
    rows = fields * radial
    half, slots = rows // 2, fwh_cell.shape[2]
    edge_shape = jax.ShapeDtypeStruct((fields, TILE, LANES), f32)

    order = ring_order(thetas)
    onward = [(order[i], order[(i + 1) % thetas]) for i in range(thetas)]
    back = [(b, a) for a, b in onward]

    across = [(order[i], order[(i + thetas // 2) % thetas]) for i in range(thetas)]
    flat = adjoint.reshape(rows, LANES)
    own = [flat[:half], flat[half:]]
    steps = thetas // 2 - 1

    from_left, from_right, halves = list(own), list(own), []
    for step in range(steps):
        left, right = [], []
        for part in range(2):
            left.append(lax.ppermute(from_left[part], "az", onward))
            right.append(lax.ppermute(from_right[part], "az", back))
        from_left, from_right = left, right
        if step == 0:
            source, from_left[0] = lax.optimization_barrier((adjoint, from_left[0]))
            last_edges = pl.pallas_call(
                edges_body,
                out_shape=edge_shape,
                in_specs=in_vmem(1),
                out_specs=in_vmem(1)[0],
                compiler_params=params,
                name="edges",
            )(source)
            last_edges = lax.ppermute(last_edges, "az", across)
        if step == 0 + 1:
            last_edges, from_right[1] = lax.optimization_barrier((last_edges, from_right[1]))
        if step == 0:
            weights = lax.dynamic_slice_in_dim(
                jnp.asarray(ring_weights(thetas)), lax.axis_index("az"), 1, axis=0
            )
            tables = pl.pallas_call(
                slots_body,
                out_shape=(
                    jax.ShapeDtypeStruct((LANES, slots), jnp.bfloat16),
                    jax.ShapeDtypeStruct((radial, slots), f32),
                    jax.ShapeDtypeStruct((devices, slots), f32),
                    jax.ShapeDtypeStruct((LANES, slots), jnp.bfloat16),
                ),
                in_specs=in_smem(1) + in_vmem(3),
                out_specs=tuple(in_vmem(4)),
                compiler_params=params,
                name="slots",
            )(fwh_count, fwh_cell, fwh_bin, fwh_weight)
        if step == 1:
            weights, tables, from_right[1] = lax.optimization_barrier(
                (weights, tables, from_right[1])
            )
        halves += from_left + from_right
    last_first = lax.ppermute(from_left[0], "az", onward)
    last_second = lax.ppermute(from_right[1], "az", back)

    blocks = len(halves) // 2
    smooth, slope, edges = pl.pallas_call(
        functools.partial(partial_body, blocks),
        out_shape=(
            jax.ShapeDtypeStruct((rows, LANES), f32),
            jax.ShapeDtypeStruct((rows, LANES), f32),
            edge_shape,
        ),
        in_specs=in_smem(1) + in_vmem(2 + 2 * blocks),
        out_specs=tuple(in_vmem(3)),
        compiler_params=params,
        name="partial",
    )(weights, adjoint, last_edges, *halves)
    pairs = [(b, b ^ 1) for b in range(blocks_x)]
    nexts = [(b, (b + (1 if b % 2 else -1)) % blocks_x) for b in range(blocks_x)]
    edges_next, edges_pair = lax.ppermute(edges, "rx", nexts), lax.ppermute(edges, "rx", pairs)
    place_x = jnp.reshape(lax.axis_index("rx"), (1, 1))

    held, totals = pl.pallas_call(
        functools.partial(final_body, blocks_x),
        out_shape=(
            jax.ShapeDtypeStruct(adjoint.shape, f32),
            jax.ShapeDtypeStruct((devices, LANES), f32),
        ),
        in_specs=in_smem(2) + in_vmem(13),
        out_specs=tuple(in_vmem(2)),
        scratch_shapes=[
            pltpu.VMEM((fields, radial + 2 * TILE, LANES), f32),
            pltpu.VMEM((fields, radial, LANES), f32),
            pltpu.VMEM((radial, LANES), f32),
        ],
        compiler_params=params,
        name="section",
    )(
        weights,
        place_x,
        smooth,
        slope,
        last_first,
        last_second,
        edges_pair,
        edges_next,
        density,
        velocity,
        pressure,
        *tables,
    )
    totals = lax.all_to_all(totals, ("az", "rx"), 0, 0, tiled=True)
    section = pl.pallas_call(
        store_body,
        out_shape=jax.ShapeDtypeStruct(adjoint.shape, f32),
        in_specs=[pl.BlockSpec(memory_space=pl.ANY)],
        out_specs=pl.BlockSpec(memory_space=pl.ANY),
        scratch_shapes=[pltpu.SemaphoreType.DMA],
        compiler_params=params,
        name="store",
    )(held)
    return section, jnp.sum(totals, axis=0)[:BIN_DEV]


def solution(mesh):
    placed = (
        P(None, "az", None, "rx"),
        P("az", None, "rx"),
        P(None, "az", None, "rx"),
        P("az", None, "rx"),
        P("az", "rx", None),
        P("az", "rx", None),
        P("az", "rx", None),
        P("az", "rx"),
    )
    return jax.shard_map(
        local,
        mesh=mesh,
        in_specs=placed,
        out_specs=(P(None, "az", None, "rx"), P(("az", "rx"))),
        check_vma=False,
    )
```

```python
import functools
import math

import jax
import jax.numpy as jnp
import numpy as np
from jax import lax
from jax.experimental import pallas as pl
from jax.experimental.pallas import tpu as pltpu
from jax.sharding import PartitionSpec as P

BIN_DEV = 8
LANES = 128
TILE = 8
EDGE = 3
SLOT = 8

ALPHA_FILTER = 0.495
COEF_ZERO = 11.0 / 16.0 + 5.0 * ALPHA_FILTER / 8.0
COEF_ONE = 15.0 / 32.0 + 17.0 * ALPHA_FILTER / 16.0
COEF_TWO = -3.0 / 16.0 + 3.0 * ALPHA_FILTER / 8.0
COEF_THREE = 1.0 / 32.0 - ALPHA_FILTER / 16.0
ALPHA_DERIV = 1.0 / 3.0
NEAR_COEF = 14.0 / 9.0
FAR_COEF = 1.0 / 9.0
AXIAL_STEP = 0.02
RADIAL_STEP = 0.02
INNER_RADIUS = 0.3
SECTION_STEP = 0.004
GAMMA_GAS = 1.4


def kernel_values(count):
    modes = np.arange(count)
    angle = modes * (2.0 * math.pi / count)
    cosine = np.cos(angle)
    filter_gain = (
        COEF_ZERO
        + COEF_ONE * cosine
        + COEF_TWO * np.cos(2.0 * angle)
        + COEF_THREE * np.cos(3.0 * angle)
    ) / (1.0 + 2.0 * ALPHA_FILTER * cosine)
    spacing = 2.0 * math.pi / count
    deriv_gain = (
        filter_gain
        * (NEAR_COEF * np.sin(angle) + 0.5 * FAR_COEF * np.sin(2.0 * angle))
        / (spacing * (1.0 + 2.0 * ALPHA_DERIV * cosine))
    )
    phase = np.mod(modes[:, None] * modes[None, :], count) * (2.0 * math.pi / count)
    smooth = np.sum(filter_gain * np.cos(phase), axis=-1) / count
    slope = -np.sum(deriv_gain * np.sin(phase), axis=-1) / count
    return smooth, slope


def ring_order(count):
    return list(range(0, count, 2)) + list(range(count - 1, 0, -2))


def ring_weights(count):
    order = ring_order(count)
    smooth, slope = kernel_values(count)
    rows = []
    for i in range(count):
        at = order.index(i)
        hops = [0]
        for s in range(1, count // 2):
            hops += [-s, s]
        hops.append(count // 2)
        away = [(i - order[(at + hop) % count]) % count for hop in hops]
        rows.append([smooth[d] for d in away] + [slope[d] for d in away])
    return np.array(rows, np.float32)


def packed_edges(tiles):
    lane = lax.broadcasted_iota(jnp.int32, (TILE, LANES), 1)
    packed = jnp.zeros((TILE, LANES), jnp.float32)
    for k, tile in enumerate(tiles):
        moved = pltpu.roll(tile, (SLOT * k + EDGE) % LANES, 1)
        packed = jnp.where(lax.shift_right_logical(lane, 3) == k, moved, packed)
    return packed


def edges_body(source, edges):
    fields, radial = source.shape[0], source.shape[2]
    for field in range(fields):
        tiles = [source[field, 0, pl.ds(row, TILE), :] for row in range(0, radial, TILE)]
        edges[field] = packed_edges(tiles)


def partial_body(blocks, weights, source, last_edges, *refs):
    count = weights.shape[1] // 2
    halves, (smooth, slope, edges) = refs[: 2 * blocks], refs[2 * blocks :]
    fields, radial = source.shape[0], source.shape[2]
    half = halves[0].shape[0]
    for field in range(fields):
        tiles = []
        for row in range(0, radial, TILE):
            at = field * radial + row
            value = source[field, 0, pl.ds(row, TILE), :]
            first, second = weights[0, 0] * value, weights[0, count] * value
            for k in range(blocks):
                value = halves[2 * k + at // half][pl.ds(at % half, TILE), :]
                first = first + weights[0, 1 + k] * value
                second = second + weights[0, count + 1 + k] * value
            smooth[pl.ds(at, TILE), :] = first
            slope[pl.ds(at, TILE), :] = second
            tiles.append(first)
        edges[field] = packed_edges(tiles) + weights[0, count - 1] * last_edges[field]


def slots_body(
    live_count,
    cells,
    bins,
    slot_weights,
    density,
    velocity,
    pressure,
    column,
    line,
    owner,
    place,
    edge_column,
    edge_line,
    flow_edges,
):
    slots, radial = cells.shape[2], density.shape[1]
    cell, own_bin = cells[0], bins[0]
    order = lax.broadcasted_iota(jnp.int32, (1, slots), 1)
    weight = jnp.where(order < live_count[0, 0], slot_weights[0], 0.0)
    x = cell & (LANES - 1)
    row = lax.shift_right_logical(cell, LANES.bit_length() - 1)

    def table(target, index, value):
        rows = lax.broadcasted_iota(jnp.int32, target.shape, 0)
        target[...] = jnp.where(rows == index, value, 0.0).astype(target.dtype)

    table(column, x, 1.0)
    table(line, row, weight)
    table(owner, own_bin // BIN_DEV, 1.0)
    table(place, own_bin % BIN_DEV, 1.0)
    base = SLOT * lax.shift_right_logical(row, TILE.bit_length() - 1)
    outer = jnp.where(x >= LANES - EDGE, base + (x - (LANES - EDGE)), -1)
    table(edge_column, jnp.where(x < EDGE, base + EDGE + x, outer), 1.0)
    table(edge_line, row & (TILE - 1), weight)
    for which, make in enumerate(
        (
            lambda rows: velocity[0, 0, rows, :],
            lambda rows: density[0, rows, :],
            lambda rows: GAMMA_GAS * pressure[0, rows, :],
            lambda rows: 1.0 / density[0, rows, :],
        )
    ):
        tiles = [make(pl.ds(at, TILE)) for at in range(0, radial, TILE)]
        flow_edges[which] = packed_edges(tiles)


def three_parts(value):
    parts = []
    for _ in range(3):
        part = value.astype(jnp.bfloat16)
        parts.append(part)
        value = value - part.astype(jnp.float32)
    return jnp.concatenate(parts, axis=0)


def add_parts(stacked):
    rows = stacked.shape[0] // 3
    return stacked[:rows] + (stacked[rows : 2 * rows] + stacked[2 * rows :])


def axial_coefs():
    unit = SECTION_STEP / (60.0 * AXIAL_STEP)
    return [np.float32(c * unit) for c in (45.0, -9.0, 1.0)]


def bulk_body(
    weights,
    smooth,
    slope,
    last_first,
    last_second,
    density,
    velocity,
    pressure,
    column,
    line,
    section,
    values,
    filtered,
    picked,
):
    fields, radial = section.shape[0], section.shape[2]
    count = weights.shape[1] // 2
    half = last_first.shape[0]
    last_weight, last_slope = weights[0, count - 1], weights[0, 2 * count - 1]

    def last(at):
        source = last_first if at < half else last_second
        return source[pl.ds(at % half, TILE), :]

    lane = lax.broadcasted_iota(jnp.int32, (TILE, LANES), 1)
    sub = lax.broadcasted_iota(jnp.int32, (TILE, LANES), 0)
    pad = jnp.zeros((TILE, LANES), jnp.float32)
    for field in range(fields):
        filtered[field, pl.ds(0, TILE), :] = pad
        filtered[field, pl.ds(TILE + radial, TILE), :] = pad
        for row in range(0, radial, TILE):
            at = field * radial + row
            value = smooth[pl.ds(at, TILE), :] + last_weight * last(at)
            filtered[field, pl.ds(TILE + row, TILE), :] = value

    axial = axial_coefs()
    unit = SECTION_STEP / (60.0 * RADIAL_STEP)
    radially = [np.float32(c * unit) for c in (45.0, -9.0, 1.0)]

    for row in range(0, radial, TILE):
        rows = pl.ds(row, TILE)
        middle, g, e, s = [], [], [], []
        cell_radius = INNER_RADIUS + ((sub + row).astype(jnp.float32) + 0.5) * RADIAL_STEP
        stretch = SECTION_STEP / cell_radius
        for field in range(fields):
            here = filtered[field, pl.ds(TILE + row, TILE), :]
            total = None
            for k in range(1, EDGE + 1):
                ahead = pltpu.roll(jnp.where(lane < k, 0.0, here), LANES - k, 1)
                behind = pltpu.roll(jnp.where(lane >= LANES - k, 0.0, here), k, 1)
                term = axial[k - 1] * (ahead - behind)
                total = term if total is None else total + term
            g.append(total)
            total = None
            for k in range(1, EDGE + 1):
                above = filtered[field, pl.ds(TILE + row + k, TILE), :]
                below = filtered[field, pl.ds(TILE + row - k, TILE), :]
                term = radially[k - 1] * (above - below)
                total = term if total is None else total + term
            e.append(total)
            at = field * radial + row
            s.append((slope[pl.ds(at, TILE), :] + last_slope * last(at)) * stretch)
            middle.append(here)
        rho = density[0, rows, :]
        u, v, w = (velocity[i, 0, rows, :] for i in range(3))
        stiff = GAMMA_GAS * pressure[0, rows, :]
        inverse = 1.0 / rho
        moved = [u * g[i] + v * e[i] + w * s[i] for i in range(fields)]
        out = [
            middle[0] + moved[0],
            middle[1] + (moved[1] + rho * g[0] + stiff * g[4]),
            middle[2] + (moved[2] + rho * e[0] + stiff * e[4]),
            middle[3] + (moved[3] + rho * s[0] + stiff * s[4]),
            middle[4] + (moved[4] + inverse * (g[1] + e[2] + s[3])),
        ]
        for field in range(fields):
            section[field, 0, rows, :] = out[field]
        picked[rows, :] = out[4] + out[1]

    lines = jnp.dot(three_parts(picked[...]), column[...], preferred_element_type=jnp.float32)
    values[...] = jnp.sum(line[...] * add_parts(lines), axis=0, keepdims=True)


def close_body(
    blocks_x,
    place_x,
    edges_pair,
    edges_next,
    flow_edges,
    values,
    edge_column,
    edge_line,
    owner,
    place,
    fixes,
    totals,
):
    fields = fixes.shape[0]
    lane = lax.broadcasted_iota(jnp.int32, (TILE, LANES), 1)
    slot = lane & (SLOT - 1)
    odd = (place_x[0, 0] & 1) == 1
    paired = (slot < EDGE) == odd
    inner = jnp.where((place_x[0, 0] == 0) | (place_x[0, 0] == blocks_x - 1), 0.0, 1.0)
    g = []
    for field in range(fields):
        halo = jnp.where(paired, edges_pair[field], inner * edges_next[field])
        total = None
        for k, coef in enumerate(axial_coefs(), 1):
            after = jnp.where(slot + k >= EDGE, pltpu.roll(halo, LANES - k, 1), 0.0)
            before = jnp.where(slot - k < EDGE, pltpu.roll(halo, k, 1), 0.0)
            term = coef * jnp.where(slot < EDGE, after, -before)
            total = term if total is None else total + term
        g.append(total)
    u, rho, stiff, inverse = (flow_edges[i] for i in range(4))
    out = [
        u * g[0],
        u * g[1] + rho * g[0] + stiff * g[4],
        u * g[2],
        u * g[3],
        u * g[4] + inverse * g[1],
    ]
    for field in range(fields):
        fixes[field] = out[field]
    seen = jnp.concatenate([out[4] + out[1], jnp.zeros((TILE, LANES), jnp.float32)], axis=0)
    lines = jnp.dot(three_parts(seen), edge_column[...], preferred_element_type=jnp.float32)
    share = jnp.sum(edge_line[...] * add_parts(lines)[:TILE], axis=0, keepdims=True)
    spread = three_parts(owner[...] * (values[...] + share))
    totals[...] = add_parts(
        lax.dot_general(
            spread, place[...], (((1,), (1,)), ((), ())), preferred_element_type=jnp.float32
        )
    )


def store_body(held, fixes, section):
    fields, radial = section.shape[0], section.shape[2]
    lane = lax.broadcasted_iota(jnp.int32, (TILE, LANES), 1)
    outer = (lane < EDGE) | (lane >= LANES - EDGE)
    for field in range(fields):
        for row in range(0, radial, TILE):
            rows = pl.ds(row, TILE)
            fix = pltpu.roll(fixes[field], LANES - (SLOT * (row // TILE) + EDGE), 1)
            section[field, 0, rows, :] = held[field, 0, rows, :] + jnp.where(outer, fix, 0.0)


def in_vmem(count):
    return [pl.BlockSpec(memory_space=pltpu.VMEM)] * count


def in_smem(count):
    return [pl.BlockSpec(memory_space=pltpu.SMEM)] * count


def local(adjoint, density, velocity, pressure, fwh_cell, fwh_bin, fwh_weight, fwh_count):
    fields, local_theta, radial, axial_cells = adjoint.shape
    thetas, blocks_x = lax.axis_size("az"), lax.axis_size("rx")
    devices = thetas * blocks_x
    assert local_theta == 1 and axial_cells == LANES and thetas % 2 == 0 and blocks_x % 2 == 0
    assert radial % TILE == 0 and radial // TILE * SLOT <= LANES
    params = pltpu.CompilerParams(vmem_limit_bytes=40 * 1024 * 1024)
    f32 = jnp.float32
    rows = fields * radial
    half, slots = rows // 2, fwh_cell.shape[2]
    edge_shape = jax.ShapeDtypeStruct((fields, TILE, LANES), f32)

    order = ring_order(thetas)
    onward = [(order[i], order[(i + 1) % thetas]) for i in range(thetas)]
    back = [(b, a) for a, b in onward]

    across = [(order[i], order[(i + thetas // 2) % thetas]) for i in range(thetas)]
    flat = adjoint.reshape(rows, LANES)
    own = [flat[:half], flat[half:]]
    steps = thetas // 2 - 1

    from_left, from_right, halves = list(own), list(own), []
    for step in range(steps):
        left, right = [], []
        for part in range(2):
            left.append(lax.ppermute(from_left[part], "az", onward))
            right.append(lax.ppermute(from_right[part], "az", back))
        from_left, from_right = left, right
        if step == 0:
            source, from_left[0] = lax.optimization_barrier((adjoint, from_left[0]))
            last_edges = pl.pallas_call(
                edges_body,
                out_shape=edge_shape,
                in_specs=in_vmem(1),
                out_specs=in_vmem(1)[0],
                compiler_params=params,
                name="edges",
            )(source)
            last_edges = lax.ppermute(last_edges, "az", across)
        if step == 0 + 1:
            last_edges, from_right[1] = lax.optimization_barrier((last_edges, from_right[1]))
        if step == 0:
            weights = lax.dynamic_slice_in_dim(
                jnp.asarray(ring_weights(thetas)), lax.axis_index("az"), 1, axis=0
            )
            tables = pl.pallas_call(
                slots_body,
                out_shape=(
                    jax.ShapeDtypeStruct((LANES, slots), jnp.bfloat16),
                    jax.ShapeDtypeStruct((radial, slots), f32),
                    jax.ShapeDtypeStruct((devices, slots), f32),
                    jax.ShapeDtypeStruct((LANES, slots), jnp.bfloat16),
                    jax.ShapeDtypeStruct((LANES, slots), jnp.bfloat16),
                    jax.ShapeDtypeStruct((TILE, slots), f32),
                    jax.ShapeDtypeStruct((4, TILE, LANES), f32),
                ),
                in_specs=in_smem(1) + in_vmem(6),
                out_specs=tuple(in_vmem(7)),
                compiler_params=params,
                name="slots",
            )(fwh_count, fwh_cell, fwh_bin, fwh_weight, density, velocity, pressure)
        if step == 1:
            weights, tables, from_right[1] = lax.optimization_barrier(
                (weights, tables, from_right[1])
            )
        halves += from_left + from_right
    last_first = lax.ppermute(from_left[0], "az", onward)
    last_second = lax.ppermute(from_right[1], "az", back)

    blocks = len(halves) // 2
    smooth, slope, edges = pl.pallas_call(
        functools.partial(partial_body, blocks),
        out_shape=(
            jax.ShapeDtypeStruct((rows, LANES), f32),
            jax.ShapeDtypeStruct((rows, LANES), f32),
            edge_shape,
        ),
        in_specs=in_smem(1) + in_vmem(2 + 2 * blocks),
        out_specs=tuple(in_vmem(3)),
        compiler_params=params,
        name="partial",
    )(weights, adjoint, last_edges, *halves)
    pairs = [(b, b ^ 1) for b in range(blocks_x)]
    nexts = [(b, (b + (1 if b % 2 else -1)) % blocks_x) for b in range(blocks_x)]
    edges_next, edges_pair = lax.ppermute(edges, "rx", nexts), lax.ppermute(edges, "rx", pairs)
    place_x = jnp.reshape(lax.axis_index("rx"), (1, 1))

    column, line, owner, place, edge_column, edge_line, flow_edges = tables
    held, values = pl.pallas_call(
        bulk_body,
        out_shape=(
            jax.ShapeDtypeStruct(adjoint.shape, f32),
            jax.ShapeDtypeStruct((1, slots), f32),
        ),
        in_specs=in_smem(1) + in_vmem(9),
        out_specs=tuple(in_vmem(2)),
        scratch_shapes=[
            pltpu.VMEM((fields, radial + 2 * TILE, LANES), f32),
            pltpu.VMEM((radial, LANES), f32),
        ],
        compiler_params=params,
        name="bulk",
    )(
        weights,
        smooth,
        slope,
        last_first,
        last_second,
        density,
        velocity,
        pressure,
        column,
        line,
    )
    fixes, totals = pl.pallas_call(
        functools.partial(close_body, blocks_x),
        out_shape=(edge_shape, jax.ShapeDtypeStruct((devices, LANES), f32)),
        in_specs=in_smem(1) + in_vmem(8),
        out_specs=tuple(in_vmem(2)),
        compiler_params=params,
        name="close",
    )(
        place_x,
        edges_pair,
        edges_next,
        flow_edges,
        values,
        edge_column,
        edge_line,
        owner,
        place,
    )
    totals = lax.all_to_all(totals, ("az", "rx"), 0, 0, tiled=True)
    section = pl.pallas_call(
        store_body,
        out_shape=jax.ShapeDtypeStruct(adjoint.shape, f32),
        in_specs=in_vmem(2),
        out_specs=in_vmem(1)[0],
        compiler_params=params,
        name="store",
    )(held, fixes)
    return section, jnp.sum(totals, axis=0)[:BIN_DEV]


def solution(mesh):
    placed = (
        P(None, "az", None, "rx"),
        P("az", None, "rx"),
        P(None, "az", None, "rx"),
        P("az", None, "rx"),
        P("az", "rx", None),
        P("az", "rx", None),
        P("az", "rx", None),
        P("az", "rx"),
    )
    return jax.shard_map(
        local,
        mesh=mesh,
        in_specs=placed,
        out_specs=(P(None, "az", None, "rx"), P(("az", "rx"))),
        check_vma=False,
    )
```

```python
import functools
import math

import jax
import jax.numpy as jnp
import numpy as np
from jax import lax
from jax.experimental import pallas as pl
from jax.experimental.pallas import tpu as pltpu
from jax.sharding import PartitionSpec as P

BIN_DEV = 8
LANES = 128
TILE = 8
EDGE = 3
SLOT = 8

ALPHA_FILTER = 0.495
COEF_ZERO = 11.0 / 16.0 + 5.0 * ALPHA_FILTER / 8.0
COEF_ONE = 15.0 / 32.0 + 17.0 * ALPHA_FILTER / 16.0
COEF_TWO = -3.0 / 16.0 + 3.0 * ALPHA_FILTER / 8.0
COEF_THREE = 1.0 / 32.0 - ALPHA_FILTER / 16.0
ALPHA_DERIV = 1.0 / 3.0
NEAR_COEF = 14.0 / 9.0
FAR_COEF = 1.0 / 9.0
AXIAL_STEP = 0.02
RADIAL_STEP = 0.02
INNER_RADIUS = 0.3
SECTION_STEP = 0.004
GAMMA_GAS = 1.4


def kernel_values(count):
    modes = np.arange(count)
    angle = modes * (2.0 * math.pi / count)
    cosine = np.cos(angle)
    filter_gain = (
        COEF_ZERO
        + COEF_ONE * cosine
        + COEF_TWO * np.cos(2.0 * angle)
        + COEF_THREE * np.cos(3.0 * angle)
    ) / (1.0 + 2.0 * ALPHA_FILTER * cosine)
    spacing = 2.0 * math.pi / count
    deriv_gain = (
        filter_gain
        * (NEAR_COEF * np.sin(angle) + 0.5 * FAR_COEF * np.sin(2.0 * angle))
        / (spacing * (1.0 + 2.0 * ALPHA_DERIV * cosine))
    )
    phase = np.mod(modes[:, None] * modes[None, :], count) * (2.0 * math.pi / count)
    smooth = np.sum(filter_gain * np.cos(phase), axis=-1) / count
    slope = -np.sum(deriv_gain * np.sin(phase), axis=-1) / count
    return smooth, slope


def ring_order(count):
    return list(range(0, count, 2)) + list(range(count - 1, 0, -2))


def ring_weights(count):
    order = ring_order(count)
    smooth, slope = kernel_values(count)
    rows = []
    for i in range(count):
        at = order.index(i)
        hops = [0]
        for s in range(1, count // 2):
            hops += [-s, s]
        hops.append(count // 2)
        away = [(i - order[(at + hop) % count]) % count for hop in hops]
        rows.append([smooth[d] for d in away] + [slope[d] for d in away])
    return np.array(rows, np.float32)


def packed_edges(tiles):
    lane = lax.broadcasted_iota(jnp.int32, (TILE, LANES), 1)
    packed = jnp.zeros((TILE, LANES), jnp.float32)
    for k, tile in enumerate(tiles):
        moved = pltpu.roll(tile, (SLOT * k + EDGE) % LANES, 1)
        packed = jnp.where(lax.shift_right_logical(lane, 3) == k, moved, packed)
    return packed


def edges_body(source, edges):
    fields, radial = source.shape[0], source.shape[2]
    for field in range(fields):
        tiles = [source[field, 0, pl.ds(row, TILE), :] for row in range(0, radial, TILE)]
        edges[field] = packed_edges(tiles)


def early_body(weights, source, *refs):
    count = weights.shape[1] // 2
    halves, (smooth, slope) = refs[:-2], refs[-2:]
    fields, radial = source.shape[0], source.shape[2]
    half = halves[0].shape[0]
    for field in range(fields):
        for row in range(0, radial, TILE):
            at = field * radial + row
            value = source[field, 0, pl.ds(row, TILE), :]
            first, second = weights[0, 0] * value, weights[0, count] * value
            for k in range(len(halves) // 2):
                value = halves[2 * k + at // half][pl.ds(at % half, TILE), :]
                first = first + weights[0, 1 + k] * value
                second = second + weights[0, count + 1 + k] * value
            smooth[pl.ds(at, TILE), :] = first
            slope[pl.ds(at, TILE), :] = second


def partial_body(
    weights,
    early_smooth,
    early_slope,
    left_first,
    left_second,
    right_first,
    right_second,
    last_edges,
    smooth,
    slope,
    edges,
):
    count, fields = weights.shape[1] // 2, edges.shape[0]
    half, radial = left_first.shape[0], smooth.shape[0] // fields
    lefts, rights = (left_first, left_second), (right_first, right_second)
    for field in range(fields):
        tiles = []
        for row in range(0, radial, TILE):
            at = field * radial + row
            rows, part = pl.ds(at, TILE), pl.ds(at % half, TILE)
            left, right = lefts[at // half][part, :], rights[at // half][part, :]
            near, far = weights[0, count - 3], weights[0, count - 2]
            tiles.append(early_smooth[rows, :] + (near * left + far * right))
            smooth[rows, :] = tiles[-1]
            near, far = weights[0, 2 * count - 3], weights[0, 2 * count - 2]
            slope[rows, :] = early_slope[rows, :] + (near * left + far * right)
        edges[field] = packed_edges(tiles) + weights[0, count - 1] * last_edges[field]


def slots_body(
    live_count,
    cells,
    bins,
    slot_weights,
    density,
    velocity,
    pressure,
    column,
    line,
    owner,
    place,
    edge_column,
    edge_line,
    flow_edges,
):
    slots, radial = cells.shape[2], density.shape[1]
    cell, own_bin = cells[0], bins[0]
    order = lax.broadcasted_iota(jnp.int32, (1, slots), 1)
    weight = jnp.where(order < live_count[0, 0], slot_weights[0], 0.0)
    x = cell & (LANES - 1)
    row = lax.shift_right_logical(cell, LANES.bit_length() - 1)

    def table(target, index, value):
        rows = lax.broadcasted_iota(jnp.int32, target.shape, 0)
        target[...] = jnp.where(rows == index, value, 0.0).astype(target.dtype)

    table(column, x, 1.0)
    table(line, row, weight)
    table(owner, own_bin // BIN_DEV, 1.0)
    table(place, own_bin % BIN_DEV, 1.0)
    base = SLOT * lax.shift_right_logical(row, TILE.bit_length() - 1)
    outer = jnp.where(x >= LANES - EDGE, base + (x - (LANES - EDGE)), -1)
    table(edge_column, jnp.where(x < EDGE, base + EDGE + x, outer), 1.0)
    table(edge_line, row & (TILE - 1), weight)
    for which, make in enumerate(
        (
            lambda rows: velocity[0, 0, rows, :],
            lambda rows: density[0, rows, :],
            lambda rows: GAMMA_GAS * pressure[0, rows, :],
            lambda rows: 1.0 / density[0, rows, :],
        )
    ):
        tiles = [make(pl.ds(at, TILE)) for at in range(0, radial, TILE)]
        flow_edges[which] = packed_edges(tiles)


def three_parts(value):
    parts = []
    for _ in range(3):
        part = value.astype(jnp.bfloat16)
        parts.append(part)
        value = value - part.astype(jnp.float32)
    return jnp.concatenate(parts, axis=0)


def add_parts(stacked):
    rows = stacked.shape[0] // 3
    return stacked[:rows] + (stacked[rows : 2 * rows] + stacked[2 * rows :])


def axial_coefs():
    unit = SECTION_STEP / (60.0 * AXIAL_STEP)
    return [np.float32(c * unit) for c in (45.0, -9.0, 1.0)]


def bulk_body(
    weights,
    smooth,
    slope,
    last_first,
    last_second,
    density,
    velocity,
    pressure,
    column,
    line,
    section,
    values,
    filtered,
    picked,
):
    fields, radial = section.shape[0], section.shape[2]
    count = weights.shape[1] // 2
    half = last_first.shape[0]
    last_weight, last_slope = weights[0, count - 1], weights[0, 2 * count - 1]

    def last(at):
        source = last_first if at < half else last_second
        return source[pl.ds(at % half, TILE), :]

    lane = lax.broadcasted_iota(jnp.int32, (TILE, LANES), 1)
    sub = lax.broadcasted_iota(jnp.int32, (TILE, LANES), 0)
    pad = jnp.zeros((TILE, LANES), jnp.float32)
    for field in range(fields):
        filtered[field, pl.ds(0, TILE), :] = pad
        filtered[field, pl.ds(TILE + radial, TILE), :] = pad
        for row in range(0, radial, TILE):
            at = field * radial + row
            value = smooth[pl.ds(at, TILE), :] + last_weight * last(at)
            filtered[field, pl.ds(TILE + row, TILE), :] = value

    axial = axial_coefs()
    unit = SECTION_STEP / (60.0 * RADIAL_STEP)
    radially = [np.float32(c * unit) for c in (45.0, -9.0, 1.0)]

    for row in range(0, radial, TILE):
        rows = pl.ds(row, TILE)
        middle, g, e, s = [], [], [], []
        cell_radius = INNER_RADIUS + ((sub + row).astype(jnp.float32) + 0.5) * RADIAL_STEP
        stretch = SECTION_STEP / cell_radius
        for field in range(fields):
            here = filtered[field, pl.ds(TILE + row, TILE), :]
            total = None
            for k in range(1, EDGE + 1):
                ahead = pltpu.roll(jnp.where(lane < k, 0.0, here), LANES - k, 1)
                behind = pltpu.roll(jnp.where(lane >= LANES - k, 0.0, here), k, 1)
                term = axial[k - 1] * (ahead - behind)
                total = term if total is None else total + term
            g.append(total)
            total = None
            for k in range(1, EDGE + 1):
                above = filtered[field, pl.ds(TILE + row + k, TILE), :]
                below = filtered[field, pl.ds(TILE + row - k, TILE), :]
                term = radially[k - 1] * (above - below)
                total = term if total is None else total + term
            e.append(total)
            at = field * radial + row
            s.append((slope[pl.ds(at, TILE), :] + last_slope * last(at)) * stretch)
            middle.append(here)
        rho = density[0, rows, :]
        u, v, w = (velocity[i, 0, rows, :] for i in range(3))
        stiff = GAMMA_GAS * pressure[0, rows, :]
        inverse = 1.0 / rho
        moved = [u * g[i] + v * e[i] + w * s[i] for i in range(fields)]
        out = [
            middle[0] + moved[0],
            middle[1] + (moved[1] + rho * g[0] + stiff * g[4]),
            middle[2] + (moved[2] + rho * e[0] + stiff * e[4]),
            middle[3] + (moved[3] + rho * s[0] + stiff * s[4]),
            middle[4] + (moved[4] + inverse * (g[1] + e[2] + s[3])),
        ]
        for field in range(fields):
            section[field, 0, rows, :] = out[field]
        picked[rows, :] = out[4] + out[1]

    lines = jnp.dot(three_parts(picked[...]), column[...], preferred_element_type=jnp.float32)
    values[...] = jnp.sum(line[...] * add_parts(lines), axis=0, keepdims=True)


def close_body(
    blocks_x,
    place_x,
    edges_next,
    edges_pair,
    flow_edges,
    values,
    edge_column,
    edge_line,
    owner,
    place,
    fixes,
    totals,
):
    fields = fixes.shape[0]
    lane = lax.broadcasted_iota(jnp.int32, (TILE, LANES), 1)
    slot = lane & (SLOT - 1)
    odd = (place_x[0, 0] & 1) == 1
    paired = (slot < EDGE) == odd
    inner = jnp.where((place_x[0, 0] == 0) | (place_x[0, 0] == blocks_x - 1), 0.0, 1.0)
    g = []
    for field in range(fields):
        halo = jnp.where(paired, edges_pair[field], inner * edges_next[field])
        total = None
        for k, coef in enumerate(axial_coefs(), 1):
            after = jnp.where(slot + k >= EDGE, pltpu.roll(halo, LANES - k, 1), 0.0)
            before = jnp.where(slot - k < EDGE, pltpu.roll(halo, k, 1), 0.0)
            term = coef * jnp.where(slot < EDGE, after, -before)
            total = term if total is None else total + term
        g.append(total)
    u, rho, stiff, inverse = (flow_edges[i] for i in range(4))
    out = [
        u * g[0],
        u * g[1] + rho * g[0] + stiff * g[4],
        u * g[2],
        u * g[3],
        u * g[4] + inverse * g[1],
    ]
    for field in range(fields):
        fixes[field] = out[field]
    seen = jnp.concatenate([out[4] + out[1], jnp.zeros((TILE, LANES), jnp.float32)], axis=0)
    lines = jnp.dot(three_parts(seen), edge_column[...], preferred_element_type=jnp.float32)
    share = jnp.sum(edge_line[...] * add_parts(lines)[:TILE], axis=0, keepdims=True)
    spread = three_parts(owner[...] * (values[...] + share))
    totals[...] = add_parts(
        lax.dot_general(
            spread, place[...], (((1,), (1,)), ((), ())), preferred_element_type=jnp.float32
        )
    )


def store_body(held, fixes, section):
    fields, radial = section.shape[0], section.shape[2]
    lane = lax.broadcasted_iota(jnp.int32, (TILE, LANES), 1)
    outer = (lane < EDGE) | (lane >= LANES - EDGE)
    for field in range(fields):
        for row in range(0, radial, TILE):
            rows = pl.ds(row, TILE)
            fix = pltpu.roll(fixes[field], LANES - (SLOT * (row // TILE) + EDGE), 1)
            section[field, 0, rows, :] = held[field, 0, rows, :] + jnp.where(outer, fix, 0.0)


def in_vmem(count):
    return [pl.BlockSpec(memory_space=pltpu.VMEM)] * count


def in_smem(count):
    return [pl.BlockSpec(memory_space=pltpu.SMEM)] * count


def local(adjoint, density, velocity, pressure, fwh_cell, fwh_bin, fwh_weight, fwh_count):
    fields, local_theta, radial, axial_cells = adjoint.shape
    thetas, blocks_x = lax.axis_size("az"), lax.axis_size("rx")
    devices = thetas * blocks_x
    assert local_theta == 1 and axial_cells == LANES and blocks_x % 2 == 0
    assert thetas % 2 == 0 and thetas >= 6
    assert radial % TILE == 0 and radial // TILE * SLOT <= LANES
    params = pltpu.CompilerParams(vmem_limit_bytes=40 * 1024 * 1024)
    f32 = jnp.float32
    rows = fields * radial
    half, slots = rows // 2, fwh_cell.shape[2]
    edge_shape = jax.ShapeDtypeStruct((fields, TILE, LANES), f32)

    order = ring_order(thetas)
    onward = [(order[i], order[(i + 1) % thetas]) for i in range(thetas)]
    back = [(b, a) for a, b in onward]

    across = [(order[i], order[(i + thetas // 2) % thetas]) for i in range(thetas)]
    flat = adjoint.reshape(rows, LANES)
    own = [flat[:half], flat[half:]]
    steps = thetas // 2 - 1

    from_left, from_right, halves = list(own), list(own), []
    for step in range(steps):
        left, right = [], []
        for part in range(2):
            left.append(lax.ppermute(from_left[part], "az", onward))
            right.append(lax.ppermute(from_right[part], "az", back))
        from_left, from_right = left, right
        if step == 0:
            source, from_left[0] = lax.optimization_barrier((adjoint, from_left[0]))
            last_edges = pl.pallas_call(
                edges_body,
                out_shape=edge_shape,
                in_specs=in_vmem(1),
                out_specs=in_vmem(1)[0],
                compiler_params=params,
                name="edges",
            )(source)
            last_edges = lax.ppermute(last_edges, "az", across)
        if step == 0 + 1:
            last_edges, from_right[1] = lax.optimization_barrier((last_edges, from_right[1]))
        if step == 0:
            weights = lax.dynamic_slice_in_dim(
                jnp.asarray(ring_weights(thetas)), lax.axis_index("az"), 1, axis=0
            )
            tables = pl.pallas_call(
                slots_body,
                out_shape=(
                    jax.ShapeDtypeStruct((LANES, slots), jnp.bfloat16),
                    jax.ShapeDtypeStruct((radial, slots), f32),
                    jax.ShapeDtypeStruct((devices, slots), f32),
                    jax.ShapeDtypeStruct((LANES, slots), jnp.bfloat16),
                    jax.ShapeDtypeStruct((LANES, slots), jnp.bfloat16),
                    jax.ShapeDtypeStruct((TILE, slots), f32),
                    jax.ShapeDtypeStruct((4, TILE, LANES), f32),
                ),
                in_specs=in_smem(1) + in_vmem(6),
                out_specs=tuple(in_vmem(7)),
                compiler_params=params,
                name="slots",
            )(fwh_count, fwh_cell, fwh_bin, fwh_weight, density, velocity, pressure)
        if step == 1:
            weights, tables, from_right[1] = lax.optimization_barrier(
                (weights, tables, from_right[1])
            )
        if step == steps - 1:
            smooth, slope, from_right[1] = lax.optimization_barrier(
                (smooth, slope, from_right[1])
            )
            continue
        halves += from_left + from_right
        if step == steps - 2:
            smooth, slope = pl.pallas_call(
                early_body,
                out_shape=(jax.ShapeDtypeStruct((rows, LANES), f32),) * 2,
                in_specs=in_smem(1) + in_vmem(1 + len(halves)),
                out_specs=tuple(in_vmem(2)),
                compiler_params=params,
                name="early",
            )(weights, adjoint, *halves)
    last_first = lax.ppermute(from_left[0], "az", onward)
    last_second = lax.ppermute(from_right[1], "az", back)

    smooth, slope, edges = pl.pallas_call(
        partial_body,
        out_shape=(jax.ShapeDtypeStruct((rows, LANES), f32),) * 2 + (edge_shape,),
        in_specs=in_smem(1) + in_vmem(7),
        out_specs=tuple(in_vmem(3)),
        compiler_params=params,
        name="partial",
    )(weights, smooth, slope, *from_left, *from_right, last_edges)
    pairs = [(b, b ^ 1) for b in range(blocks_x)]
    nexts = [(b, (b + (1 if b % 2 else -1)) % blocks_x) for b in range(blocks_x)]
    edges_next, edges_pair = lax.ppermute(edges, "rx", nexts), lax.ppermute(edges, "rx", pairs)
    place_x = jnp.reshape(lax.axis_index("rx"), (1, 1))

    column, line, owner, place, edge_column, edge_line, flow_edges = tables
    held, values = pl.pallas_call(
        bulk_body,
        out_shape=(
            jax.ShapeDtypeStruct(adjoint.shape, f32),
            jax.ShapeDtypeStruct((1, slots), f32),
        ),
        in_specs=in_smem(1) + in_vmem(9),
        out_specs=tuple(in_vmem(2)),
        scratch_shapes=[
            pltpu.VMEM((fields, radial + 2 * TILE, LANES), f32),
            pltpu.VMEM((radial, LANES), f32),
        ],
        compiler_params=params,
        name="bulk",
    )(
        weights,
        smooth,
        slope,
        last_first,
        last_second,
        density,
        velocity,
        pressure,
        column,
        line,
    )
    fixes, totals = pl.pallas_call(
        functools.partial(close_body, blocks_x),
        out_shape=(edge_shape, jax.ShapeDtypeStruct((devices, LANES), f32)),
        in_specs=in_smem(1) + in_vmem(8),
        out_specs=tuple(in_vmem(2)),
        compiler_params=params,
        name="close",
    )(
        place_x,
        edges_next,
        edges_pair,
        flow_edges,
        values,
        edge_column,
        edge_line,
        owner,
        place,
    )
    totals = lax.all_to_all(totals, ("az", "rx"), 0, 0, tiled=True)
    section = pl.pallas_call(
        store_body,
        out_shape=jax.ShapeDtypeStruct(adjoint.shape, f32),
        in_specs=in_vmem(2),
        out_specs=in_vmem(1)[0],
        compiler_params=params,
        name="store",
    )(held, fixes)
    return section, jnp.sum(totals, axis=0)[:BIN_DEV]


def solution(mesh):
    placed = (
        P(None, "az", None, "rx"),
        P("az", None, "rx"),
        P(None, "az", None, "rx"),
        P("az", None, "rx"),
        P("az", "rx", None),
        P("az", "rx", None),
        P("az", "rx", None),
        P("az", "rx"),
    )
    return jax.shard_map(
        local,
        mesh=mesh,
        in_specs=placed,
        out_specs=(P(None, "az", None, "rx"), P(("az", "rx"))),
        check_vma=False,
    )
```

```python
import functools
import math

import jax
import jax.numpy as jnp
import numpy as np
from jax import lax
from jax.experimental import pallas as pl
from jax.experimental.pallas import tpu as pltpu
from jax.sharding import PartitionSpec as P

BIN_DEV = 8
LANES = 128
TILE = 8
EDGE = 3
SLOT = 8

ALPHA_FILTER = 0.495
COEF_ZERO = 11.0 / 16.0 + 5.0 * ALPHA_FILTER / 8.0
COEF_ONE = 15.0 / 32.0 + 17.0 * ALPHA_FILTER / 16.0
COEF_TWO = -3.0 / 16.0 + 3.0 * ALPHA_FILTER / 8.0
COEF_THREE = 1.0 / 32.0 - ALPHA_FILTER / 16.0
ALPHA_DERIV = 1.0 / 3.0
NEAR_COEF = 14.0 / 9.0
FAR_COEF = 1.0 / 9.0
AXIAL_STEP = 0.02
RADIAL_STEP = 0.02
INNER_RADIUS = 0.3
SECTION_STEP = 0.004
GAMMA_GAS = 1.4


def kernel_values(count):
    modes = np.arange(count)
    angle = modes * (2.0 * math.pi / count)
    cosine = np.cos(angle)
    filter_gain = (
        COEF_ZERO
        + COEF_ONE * cosine
        + COEF_TWO * np.cos(2.0 * angle)
        + COEF_THREE * np.cos(3.0 * angle)
    ) / (1.0 + 2.0 * ALPHA_FILTER * cosine)
    spacing = 2.0 * math.pi / count
    deriv_gain = (
        filter_gain
        * (NEAR_COEF * np.sin(angle) + 0.5 * FAR_COEF * np.sin(2.0 * angle))
        / (spacing * (1.0 + 2.0 * ALPHA_DERIV * cosine))
    )
    phase = np.mod(modes[:, None] * modes[None, :], count) * (2.0 * math.pi / count)
    smooth = np.sum(filter_gain * np.cos(phase), axis=-1) / count
    slope = -np.sum(deriv_gain * np.sin(phase), axis=-1) / count
    return smooth, slope


def ring_order(count):
    return list(range(0, count, 2)) + list(range(count - 1, 0, -2))


def ring_weights(count):
    order = ring_order(count)
    smooth, slope = kernel_values(count)
    rows = []
    for i in range(count):
        at = order.index(i)
        hops = [0]
        for s in range(1, count // 2):
            hops += [-s, s]
        hops.append(count // 2)
        away = [(i - order[(at + hop) % count]) % count for hop in hops]
        rows.append([smooth[d] for d in away] + [slope[d] for d in away])
    return np.array(rows, np.float32)


def packed_edges(tiles):
    lane = lax.broadcasted_iota(jnp.int32, (TILE, LANES), 1)
    packed = jnp.zeros((TILE, LANES), jnp.float32)
    for k, tile in enumerate(tiles):
        moved = pltpu.roll(tile, (SLOT * k + EDGE) % LANES, 1)
        packed = jnp.where(lax.shift_right_logical(lane, 3) == k, moved, packed)
    return packed


def edges_body(source, edges):
    fields, radial = source.shape[0], source.shape[2]
    for field in range(fields):
        tiles = [source[field, 0, pl.ds(row, TILE), :] for row in range(0, radial, TILE)]
        edges[field] = packed_edges(tiles)


def early_body(weights, source, *refs):
    count = weights.shape[1] // 2
    halves, (smooth, slope) = refs[:-2], refs[-2:]
    fields, radial = source.shape[0], source.shape[2]
    half = halves[0].shape[0]
    for field in range(fields):
        for row in range(0, radial, TILE):
            at = field * radial + row
            value = source[field, 0, pl.ds(row, TILE), :]
            first, second = weights[0, 0] * value, weights[0, count] * value
            for k in range(len(halves) // 2):
                value = halves[2 * k + at // half][pl.ds(at % half, TILE), :]
                first = first + weights[0, 1 + k] * value
                second = second + weights[0, count + 1 + k] * value
            smooth[pl.ds(at, TILE), :] = first
            slope[pl.ds(at, TILE), :] = second


def partial_body(
    weights,
    early_smooth,
    early_slope,
    left_first,
    left_second,
    right_first,
    right_second,
    last_edges,
    smooth,
    slope,
    edges,
):
    count, fields = weights.shape[1] // 2, edges.shape[0]
    half, radial = left_first.shape[0], smooth.shape[0] // fields
    lefts, rights = (left_first, left_second), (right_first, right_second)
    for field in range(fields):
        tiles = []
        for row in range(0, radial, TILE):
            at = field * radial + row
            rows, part = pl.ds(at, TILE), pl.ds(at % half, TILE)
            left, right = lefts[at // half][part, :], rights[at // half][part, :]
            near, far = weights[0, count - 3], weights[0, count - 2]
            tiles.append(early_smooth[rows, :] + (near * left + far * right))
            smooth[rows, :] = tiles[-1]
            near, far = weights[0, 2 * count - 3], weights[0, 2 * count - 2]
            slope[rows, :] = early_slope[rows, :] + (near * left + far * right)
        edges[field] = packed_edges(tiles) + weights[0, count - 1] * last_edges[field]


def slots_body(
    live_count,
    cells,
    bins,
    slot_weights,
    density,
    velocity,
    pressure,
    column,
    line,
    owner,
    place,
    edge_column,
    edge_line,
    flow_edges,
):
    slots, radial = cells.shape[2], density.shape[1]
    cell, own_bin = cells[0], bins[0]
    order = lax.broadcasted_iota(jnp.int32, (1, slots), 1)
    weight = jnp.where(order < live_count[0, 0], slot_weights[0], 0.0)
    x = cell & (LANES - 1)
    row = lax.shift_right_logical(cell, LANES.bit_length() - 1)

    def table(target, index, value):
        rows = lax.broadcasted_iota(jnp.int32, target.shape, 0)
        target[...] = jnp.where(rows == index, value, 0.0).astype(target.dtype)

    table(column, x, 1.0)
    table(line, row, weight)
    table(owner, own_bin // BIN_DEV, 1.0)
    table(place, own_bin % BIN_DEV, 1.0)
    base = SLOT * lax.shift_right_logical(row, TILE.bit_length() - 1)
    outer = jnp.where(x >= LANES - EDGE, base + (x - (LANES - EDGE)), -1)
    table(edge_column, jnp.where(x < EDGE, base + EDGE + x, outer), 1.0)
    table(edge_line, row & (TILE - 1), weight)
    for which, make in enumerate(
        (
            lambda rows: velocity[0, 0, rows, :],
            lambda rows: density[0, rows, :],
            lambda rows: GAMMA_GAS * pressure[0, rows, :],
            lambda rows: 1.0 / density[0, rows, :],
        )
    ):
        tiles = [make(pl.ds(at, TILE)) for at in range(0, radial, TILE)]
        flow_edges[which] = packed_edges(tiles)


def three_parts(value):
    parts = []
    for _ in range(3):
        part = value.astype(jnp.bfloat16)
        parts.append(part)
        value = value - part.astype(jnp.float32)
    return jnp.concatenate(parts, axis=0)


def add_parts(stacked):
    rows = stacked.shape[0] // 3
    return stacked[:rows] + (stacked[rows : 2 * rows] + stacked[2 * rows :])


def axial_coefs():
    unit = SECTION_STEP / (60.0 * AXIAL_STEP)
    return [np.float32(c * unit) for c in (45.0, -9.0, 1.0)]


def bulk_body(
    weights,
    smooth,
    slope,
    last_first,
    last_second,
    density,
    velocity,
    pressure,
    column,
    line,
    section,
    values,
    filtered,
    picked,
):
    fields, radial = section.shape[0], section.shape[2]
    count = weights.shape[1] // 2
    half = last_first.shape[0]
    last_weight, last_slope = weights[0, count - 1], weights[0, 2 * count - 1]

    def last(at):
        source = last_first if at < half else last_second
        return source[pl.ds(at % half, TILE), :]

    lane = lax.broadcasted_iota(jnp.int32, (TILE, LANES), 1)
    sub = lax.broadcasted_iota(jnp.int32, (TILE, LANES), 0)
    pad = jnp.zeros((TILE, LANES), jnp.float32)
    for field in range(fields):
        filtered[field, pl.ds(0, TILE), :] = pad
        filtered[field, pl.ds(TILE + radial, TILE), :] = pad
        for row in range(0, radial, TILE):
            at = field * radial + row
            value = smooth[pl.ds(at, TILE), :] + last_weight * last(at)
            filtered[field, pl.ds(TILE + row, TILE), :] = value

    axial = axial_coefs()
    unit = SECTION_STEP / (60.0 * RADIAL_STEP)
    radially = [np.float32(c * unit) for c in (45.0, -9.0, 1.0)]

    for row in range(0, radial, TILE):
        rows = pl.ds(row, TILE)
        middle, g, e, s = [], [], [], []
        cell_radius = INNER_RADIUS + ((sub + row).astype(jnp.float32) + 0.5) * RADIAL_STEP
        stretch = SECTION_STEP / cell_radius
        for field in range(fields):
            here = filtered[field, pl.ds(TILE + row, TILE), :]
            total = None
            for k in range(1, EDGE + 1):
                ahead = pltpu.roll(jnp.where(lane < k, 0.0, here), LANES - k, 1)
                behind = pltpu.roll(jnp.where(lane >= LANES - k, 0.0, here), k, 1)
                term = axial[k - 1] * (ahead - behind)
                total = term if total is None else total + term
            g.append(total)
            total = None
            for k in range(1, EDGE + 1):
                above = filtered[field, pl.ds(TILE + row + k, TILE), :]
                below = filtered[field, pl.ds(TILE + row - k, TILE), :]
                term = radially[k - 1] * (above - below)
                total = term if total is None else total + term
            e.append(total)
            at = field * radial + row
            s.append((slope[pl.ds(at, TILE), :] + last_slope * last(at)) * stretch)
            middle.append(here)
        rho = density[0, rows, :]
        u, v, w = (velocity[i, 0, rows, :] for i in range(3))
        stiff = GAMMA_GAS * pressure[0, rows, :]
        inverse = 1.0 / rho
        moved = [u * g[i] + v * e[i] + w * s[i] for i in range(fields)]
        out = [
            middle[0] + moved[0],
            middle[1] + (moved[1] + rho * g[0] + stiff * g[4]),
            middle[2] + (moved[2] + rho * e[0] + stiff * e[4]),
            middle[3] + (moved[3] + rho * s[0] + stiff * s[4]),
            middle[4] + (moved[4] + inverse * (g[1] + e[2] + s[3])),
        ]
        for field in range(fields):
            section[field, 0, rows, :] = out[field]
        picked[rows, :] = out[4] + out[1]

    lines = jnp.dot(three_parts(picked[...]), column[...], preferred_element_type=jnp.float32)
    values[...] = jnp.sum(line[...] * add_parts(lines), axis=0, keepdims=True)


def close_body(
    blocks_x,
    place_x,
    edges_next,
    edges_pair,
    flow_edges,
    values,
    edge_column,
    edge_line,
    owner,
    place,
    fixes,
    totals,
):
    fields = fixes.shape[0]
    lane = lax.broadcasted_iota(jnp.int32, (TILE, LANES), 1)
    slot = lane & (SLOT - 1)
    odd = (place_x[0, 0] & 1) == 1
    paired = (slot < EDGE) == odd
    inner = jnp.where((place_x[0, 0] == 0) | (place_x[0, 0] == blocks_x - 1), 0.0, 1.0)
    g = []
    for field in range(fields):
        halo = jnp.where(paired, edges_pair[field], inner * edges_next[field])
        total = None
        for k, coef in enumerate(axial_coefs(), 1):
            after = jnp.where(slot + k >= EDGE, pltpu.roll(halo, LANES - k, 1), 0.0)
            before = jnp.where(slot - k < EDGE, pltpu.roll(halo, k, 1), 0.0)
            term = coef * jnp.where(slot < EDGE, after, -before)
            total = term if total is None else total + term
        g.append(total)
    u, rho, stiff, inverse = (flow_edges[i] for i in range(4))
    out = [
        u * g[0],
        u * g[1] + rho * g[0] + stiff * g[4],
        u * g[2],
        u * g[3],
        u * g[4] + inverse * g[1],
    ]
    for field in range(fields):
        fixes[field] = out[field]
    seen = jnp.concatenate([out[4] + out[1], jnp.zeros((TILE, LANES), jnp.float32)], axis=0)
    lines = jnp.dot(three_parts(seen), edge_column[...], preferred_element_type=jnp.float32)
    share = jnp.sum(edge_line[...] * add_parts(lines)[:TILE], axis=0, keepdims=True)
    spread = three_parts(owner[...] * (values[...] + share))
    totals[...] = add_parts(
        lax.dot_general(
            spread, place[...], (((1,), (1,)), ((), ())), preferred_element_type=jnp.float32
        )
    )


def store_body(held, fixes, totals, section, signal):
    sums = jnp.sum(totals[...], axis=0, keepdims=True)
    signal[...] = sums[0, : signal.shape[0]]
    fields, radial = section.shape[0], section.shape[2]
    lane = lax.broadcasted_iota(jnp.int32, (TILE, LANES), 1)
    outer = (lane < EDGE) | (lane >= LANES - EDGE)
    for field in range(fields):
        for row in range(0, radial, TILE):
            rows = pl.ds(row, TILE)
            fix = pltpu.roll(fixes[field], LANES - (SLOT * (row // TILE) + EDGE), 1)
            section[field, 0, rows, :] = held[field, 0, rows, :] + jnp.where(outer, fix, 0.0)


def in_vmem(count):
    return [pl.BlockSpec(memory_space=pltpu.VMEM)] * count


def in_smem(count):
    return [pl.BlockSpec(memory_space=pltpu.SMEM)] * count


def local(adjoint, density, velocity, pressure, fwh_cell, fwh_bin, fwh_weight, fwh_count):
    fields, local_theta, radial, axial_cells = adjoint.shape
    thetas, blocks_x = lax.axis_size("az"), lax.axis_size("rx")
    devices = thetas * blocks_x
    assert local_theta == 1 and axial_cells == LANES and blocks_x % 2 == 0
    assert thetas % 2 == 0 and thetas >= 6
    assert radial % TILE == 0 and radial // TILE * SLOT <= LANES
    params = pltpu.CompilerParams(vmem_limit_bytes=40 * 1024 * 1024)
    f32 = jnp.float32
    rows = fields * radial
    half, slots = rows // 2, fwh_cell.shape[2]
    edge_shape = jax.ShapeDtypeStruct((fields, TILE, LANES), f32)

    order = ring_order(thetas)
    onward = [(order[i], order[(i + 1) % thetas]) for i in range(thetas)]
    back = [(b, a) for a, b in onward]

    across = [(order[i], order[(i + thetas // 2) % thetas]) for i in range(thetas)]
    flat = adjoint.reshape(rows, LANES)
    own = [flat[:half], flat[half:]]
    steps = thetas // 2 - 1

    from_left, from_right, halves = list(own), list(own), []
    for step in range(steps):
        left, right = [], []
        for part in range(2):
            left.append(lax.ppermute(from_left[part], "az", onward))
            right.append(lax.ppermute(from_right[part], "az", back))
        from_left, from_right = left, right
        if step == 0:
            source, from_left[0] = lax.optimization_barrier((adjoint, from_left[0]))
            last_edges = pl.pallas_call(
                edges_body,
                out_shape=edge_shape,
                in_specs=in_vmem(1),
                out_specs=in_vmem(1)[0],
                compiler_params=params,
                name="edges",
            )(source)
            last_edges = lax.ppermute(last_edges, "az", across)
        if step == 0 + 1:
            last_edges, from_right[1] = lax.optimization_barrier((last_edges, from_right[1]))
        if step == 0:
            weights = lax.dynamic_slice_in_dim(
                jnp.asarray(ring_weights(thetas)), lax.axis_index("az"), 1, axis=0
            )
            tables = pl.pallas_call(
                slots_body,
                out_shape=(
                    jax.ShapeDtypeStruct((LANES, slots), jnp.bfloat16),
                    jax.ShapeDtypeStruct((radial, slots), f32),
                    jax.ShapeDtypeStruct((devices, slots), f32),
                    jax.ShapeDtypeStruct((LANES, slots), jnp.bfloat16),
                    jax.ShapeDtypeStruct((LANES, slots), jnp.bfloat16),
                    jax.ShapeDtypeStruct((TILE, slots), f32),
                    jax.ShapeDtypeStruct((4, TILE, LANES), f32),
                ),
                in_specs=in_smem(1) + in_vmem(6),
                out_specs=tuple(in_vmem(7)),
                compiler_params=params,
                name="slots",
            )(fwh_count, fwh_cell, fwh_bin, fwh_weight, density, velocity, pressure)
        if step == 1:
            weights, tables, from_right[1] = lax.optimization_barrier(
                (weights, tables, from_right[1])
            )
        if step == steps - 1:
            smooth, slope, from_right[1] = lax.optimization_barrier(
                (smooth, slope, from_right[1])
            )
            continue
        halves += from_left + from_right
        if step == steps - 2:
            smooth, slope = pl.pallas_call(
                early_body,
                out_shape=(jax.ShapeDtypeStruct((rows, LANES), f32),) * 2,
                in_specs=in_smem(1) + in_vmem(1 + len(halves)),
                out_specs=tuple(in_vmem(2)),
                compiler_params=params,
                name="early",
            )(weights, adjoint, *halves)
    last_first = lax.ppermute(from_left[0], "az", onward)
    last_second = lax.ppermute(from_right[1], "az", back)

    smooth, slope, edges = pl.pallas_call(
        partial_body,
        out_shape=(jax.ShapeDtypeStruct((rows, LANES), f32),) * 2 + (edge_shape,),
        in_specs=in_smem(1) + in_vmem(7),
        out_specs=tuple(in_vmem(3)),
        compiler_params=params,
        name="partial",
    )(weights, smooth, slope, *from_left, *from_right, last_edges)
    pairs = [(b, b ^ 1) for b in range(blocks_x)]
    nexts = [(b, (b + (1 if b % 2 else -1)) % blocks_x) for b in range(blocks_x)]
    edges_next, edges_pair = lax.ppermute(edges, "rx", nexts), lax.ppermute(edges, "rx", pairs)
    place_x = jnp.reshape(lax.axis_index("rx"), (1, 1))

    column, line, owner, place, edge_column, edge_line, flow_edges = tables
    held, values = pl.pallas_call(
        bulk_body,
        out_shape=(
            jax.ShapeDtypeStruct(adjoint.shape, f32),
            jax.ShapeDtypeStruct((1, slots), f32),
        ),
        in_specs=in_smem(1) + in_vmem(9),
        out_specs=tuple(in_vmem(2)),
        scratch_shapes=[
            pltpu.VMEM((fields, radial + 2 * TILE, LANES), f32),
            pltpu.VMEM((radial, LANES), f32),
        ],
        compiler_params=params,
        name="bulk",
    )(
        weights,
        smooth,
        slope,
        last_first,
        last_second,
        density,
        velocity,
        pressure,
        column,
        line,
    )
    fixes, totals = pl.pallas_call(
        functools.partial(close_body, blocks_x),
        out_shape=(edge_shape, jax.ShapeDtypeStruct((devices, LANES), f32)),
        in_specs=in_smem(1) + in_vmem(8),
        out_specs=tuple(in_vmem(2)),
        compiler_params=params,
        name="close",
    )(
        place_x,
        edges_next,
        edges_pair,
        flow_edges,
        values,
        edge_column,
        edge_line,
        owner,
        place,
    )
    totals = lax.all_to_all(totals, ("az", "rx"), 0, 0, tiled=True)
    section, signal = pl.pallas_call(
        store_body,
        out_shape=(
            jax.ShapeDtypeStruct(adjoint.shape, f32),
            jax.ShapeDtypeStruct((BIN_DEV,), f32),
        ),
        in_specs=in_vmem(3),
        out_specs=tuple(in_vmem(2)),
        compiler_params=params,
        name="store",
    )(held, fixes, totals)
    return section, signal


def solution(mesh):
    placed = (
        P(None, "az", None, "rx"),
        P("az", None, "rx"),
        P(None, "az", None, "rx"),
        P("az", None, "rx"),
        P("az", "rx", None),
        P("az", "rx", None),
        P("az", "rx", None),
        P("az", "rx"),
    )
    return jax.shard_map(
        local,
        mesh=mesh,
        in_specs=placed,
        out_specs=(P(None, "az", None, "rx"), P(("az", "rx"))),
        check_vma=False,
    )
```

```python
import functools
import math

import jax
import jax.numpy as jnp
import numpy as np
from jax import lax
from jax.experimental import pallas as pl
from jax.experimental.pallas import tpu as pltpu
from jax.sharding import PartitionSpec as P

BIN_DEV = 8
LANES = 128
TILE = 8
EDGE = 3
SLOT = 8

ALPHA_FILTER = 0.495
COEF_ZERO = 11.0 / 16.0 + 5.0 * ALPHA_FILTER / 8.0
COEF_ONE = 15.0 / 32.0 + 17.0 * ALPHA_FILTER / 16.0
COEF_TWO = -3.0 / 16.0 + 3.0 * ALPHA_FILTER / 8.0
COEF_THREE = 1.0 / 32.0 - ALPHA_FILTER / 16.0
ALPHA_DERIV = 1.0 / 3.0
NEAR_COEF = 14.0 / 9.0
FAR_COEF = 1.0 / 9.0
AXIAL_STEP = 0.02
RADIAL_STEP = 0.02
INNER_RADIUS = 0.3
SECTION_STEP = 0.004
GAMMA_GAS = 1.4


def kernel_values(count):
    modes = np.arange(count)
    angle = modes * (2.0 * math.pi / count)
    cosine = np.cos(angle)
    filter_gain = (
        COEF_ZERO
        + COEF_ONE * cosine
        + COEF_TWO * np.cos(2.0 * angle)
        + COEF_THREE * np.cos(3.0 * angle)
    ) / (1.0 + 2.0 * ALPHA_FILTER * cosine)
    spacing = 2.0 * math.pi / count
    deriv_gain = (
        filter_gain
        * (NEAR_COEF * np.sin(angle) + 0.5 * FAR_COEF * np.sin(2.0 * angle))
        / (spacing * (1.0 + 2.0 * ALPHA_DERIV * cosine))
    )
    phase = np.mod(modes[:, None] * modes[None, :], count) * (2.0 * math.pi / count)
    smooth = np.sum(filter_gain * np.cos(phase), axis=-1) / count
    slope = -np.sum(deriv_gain * np.sin(phase), axis=-1) / count
    return smooth, slope


def ring_order(count):
    return list(range(0, count, 2)) + list(range(count - 1, 0, -2))


def ring_weights(count):
    order = ring_order(count)
    smooth, slope = kernel_values(count)
    rows = []
    for i in range(count):
        at = order.index(i)
        hops = [0]
        for s in range(1, count // 2):
            hops += [-s, s]
        hops.append(count // 2)
        away = [(i - order[(at + hop) % count]) % count for hop in hops]
        rows.append([smooth[d] for d in away] + [slope[d] for d in away])
    return np.array(rows, np.float32)


def packed_edges(tiles):
    lane = lax.broadcasted_iota(jnp.int32, (TILE, LANES), 1)
    packed = jnp.zeros((TILE, LANES), jnp.float32)
    for k, tile in enumerate(tiles):
        moved = pltpu.roll(tile, (SLOT * k + EDGE) % LANES, 1)
        packed = jnp.where(lax.shift_right_logical(lane, 3) == k, moved, packed)
    return packed


def edges_body(source, edges):
    fields, radial = source.shape[0], source.shape[2]
    for field in range(fields):
        tiles = [source[field, 0, pl.ds(row, TILE), :] for row in range(0, radial, TILE)]
        edges[field] = packed_edges(tiles)


def early_body(weights, source, *refs):
    count = weights.shape[1] // 2
    halves, (smooth, slope, spread) = refs[:-3], refs[-3:]
    for k in range(2 * count):
        spread[k] = jnp.full((TILE, LANES), weights[0, k], jnp.float32)
    fields, radial = source.shape[0], source.shape[2]
    half = halves[0].shape[0]
    for field in range(fields):
        for row in range(0, radial, TILE):
            at = field * radial + row
            value = source[field, 0, pl.ds(row, TILE), :]
            first, second = weights[0, 0] * value, weights[0, count] * value
            for k in range(len(halves) // 2):
                value = halves[2 * k + at // half][pl.ds(at % half, TILE), :]
                first = first + weights[0, 1 + k] * value
                second = second + weights[0, count + 1 + k] * value
            smooth[pl.ds(at, TILE), :] = first
            slope[pl.ds(at, TILE), :] = second


def partial_body(
    weights,
    early_smooth,
    early_slope,
    left_first,
    left_second,
    right_first,
    right_second,
    last_edges,
    smooth,
    slope,
    edges,
):
    count, fields = weights.shape[0] // 2, edges.shape[0]
    half, radial = left_first.shape[0], smooth.shape[0] // fields
    lefts, rights = (left_first, left_second), (right_first, right_second)
    for field in range(fields):
        tiles = []
        for row in range(0, radial, TILE):
            at = field * radial + row
            rows, part = pl.ds(at, TILE), pl.ds(at % half, TILE)
            left, right = lefts[at // half][part, :], rights[at // half][part, :]
            near, far = weights[count - 3], weights[count - 2]
            tiles.append(early_smooth[rows, :] + (near * left + far * right))
            smooth[rows, :] = tiles[-1]
            near, far = weights[2 * count - 3], weights[2 * count - 2]
            slope[rows, :] = early_slope[rows, :] + (near * left + far * right)
        edges[field] = packed_edges(tiles) + weights[count - 1] * last_edges[field]


def slots_body(
    live_count,
    cells,
    bins,
    slot_weights,
    density,
    velocity,
    pressure,
    column,
    line,
    owner,
    place,
    edge_column,
    edge_line,
    flow_edges,
):
    slots, radial = cells.shape[2], density.shape[1]
    cell, own_bin = cells[0], bins[0]
    order = lax.broadcasted_iota(jnp.int32, (1, slots), 1)
    weight = jnp.where(order < live_count[0, 0], slot_weights[0], 0.0)
    x = cell & (LANES - 1)
    row = lax.shift_right_logical(cell, LANES.bit_length() - 1)

    def table(target, index, value):
        rows = lax.broadcasted_iota(jnp.int32, target.shape, 0)
        target[...] = jnp.where(rows == index, value, 0.0).astype(target.dtype)

    table(column, x, 1.0)
    table(line, row, weight)
    table(owner, own_bin // BIN_DEV, 1.0)
    table(place, own_bin % BIN_DEV, 1.0)
    base = SLOT * lax.shift_right_logical(row, TILE.bit_length() - 1)
    outer = jnp.where(x >= LANES - EDGE, base + (x - (LANES - EDGE)), -1)
    table(edge_column, jnp.where(x < EDGE, base + EDGE + x, outer), 1.0)
    table(edge_line, row & (TILE - 1), weight)
    for which, make in enumerate(
        (
            lambda rows: velocity[0, 0, rows, :],
            lambda rows: density[0, rows, :],
            lambda rows: GAMMA_GAS * pressure[0, rows, :],
            lambda rows: 1.0 / density[0, rows, :],
        )
    ):
        tiles = [make(pl.ds(at, TILE)) for at in range(0, radial, TILE)]
        flow_edges[which] = packed_edges(tiles)


def three_parts(value):
    parts = []
    for _ in range(3):
        part = value.astype(jnp.bfloat16)
        parts.append(part)
        value = value - part.astype(jnp.float32)
    return jnp.concatenate(parts, axis=0)


def add_parts(stacked):
    rows = stacked.shape[0] // 3
    return stacked[:rows] + (stacked[rows : 2 * rows] + stacked[2 * rows :])


def axial_coefs():
    unit = SECTION_STEP / (60.0 * AXIAL_STEP)
    return [np.float32(c * unit) for c in (45.0, -9.0, 1.0)]


def bulk_body(
    weights,
    smooth,
    slope,
    last_first,
    last_second,
    density,
    velocity,
    pressure,
    column,
    line,
    section,
    values,
    filtered,
    picked,
):
    fields, radial = section.shape[0], section.shape[2]
    count = weights.shape[0] // 2
    half = last_first.shape[0]
    last_weight, last_slope = weights[count - 1], weights[2 * count - 1]

    def last(at):
        source = last_first if at < half else last_second
        return source[pl.ds(at % half, TILE), :]

    lane = lax.broadcasted_iota(jnp.int32, (TILE, LANES), 1)
    sub = lax.broadcasted_iota(jnp.int32, (TILE, LANES), 0)
    pad = jnp.zeros((TILE, LANES), jnp.float32)
    for field in range(fields):
        filtered[field, pl.ds(0, TILE), :] = pad
        filtered[field, pl.ds(TILE + radial, TILE), :] = pad
        for row in range(0, radial, TILE):
            at = field * radial + row
            value = smooth[pl.ds(at, TILE), :] + last_weight * last(at)
            filtered[field, pl.ds(TILE + row, TILE), :] = value

    axial = axial_coefs()
    unit = SECTION_STEP / (60.0 * RADIAL_STEP)
    radially = [np.float32(c * unit) for c in (45.0, -9.0, 1.0)]

    for row in range(0, radial, TILE):
        rows = pl.ds(row, TILE)
        middle, g, e, s = [], [], [], []
        cell_radius = INNER_RADIUS + ((sub + row).astype(jnp.float32) + 0.5) * RADIAL_STEP
        stretch = SECTION_STEP / cell_radius
        for field in range(fields):
            here = filtered[field, pl.ds(TILE + row, TILE), :]
            total = None
            for k in range(1, EDGE + 1):
                ahead = pltpu.roll(jnp.where(lane < k, 0.0, here), LANES - k, 1)
                behind = pltpu.roll(jnp.where(lane >= LANES - k, 0.0, here), k, 1)
                term = axial[k - 1] * (ahead - behind)
                total = term if total is None else total + term
            g.append(total)
            total = None
            for k in range(1, EDGE + 1):
                above = filtered[field, pl.ds(TILE + row + k, TILE), :]
                below = filtered[field, pl.ds(TILE + row - k, TILE), :]
                term = radially[k - 1] * (above - below)
                total = term if total is None else total + term
            e.append(total)
            at = field * radial + row
            s.append((slope[pl.ds(at, TILE), :] + last_slope * last(at)) * stretch)
            middle.append(here)
        rho = density[0, rows, :]
        u, v, w = (velocity[i, 0, rows, :] for i in range(3))
        stiff = GAMMA_GAS * pressure[0, rows, :]
        inverse = 1.0 / rho
        moved = [u * g[i] + v * e[i] + w * s[i] for i in range(fields)]
        out = [
            middle[0] + moved[0],
            middle[1] + (moved[1] + rho * g[0] + stiff * g[4]),
            middle[2] + (moved[2] + rho * e[0] + stiff * e[4]),
            middle[3] + (moved[3] + rho * s[0] + stiff * s[4]),
            middle[4] + (moved[4] + inverse * (g[1] + e[2] + s[3])),
        ]
        for field in range(fields):
            section[field, 0, rows, :] = out[field]
        picked[rows, :] = out[4] + out[1]

    lines = jnp.dot(three_parts(picked[...]), column[...], preferred_element_type=jnp.float32)
    values[...] = jnp.sum(line[...] * add_parts(lines), axis=0, keepdims=True)


def close_body(
    blocks_x,
    place_x,
    edges_next,
    edges_pair,
    flow_edges,
    values,
    edge_column,
    edge_line,
    owner,
    place,
    fixes,
    totals,
):
    fields = fixes.shape[0]
    lane = lax.broadcasted_iota(jnp.int32, (TILE, LANES), 1)
    slot = lane & (SLOT - 1)
    odd = (place_x[0, 0] & 1) == 1
    paired = (slot < EDGE) == odd
    inner = jnp.where((place_x[0, 0] == 0) | (place_x[0, 0] == blocks_x - 1), 0.0, 1.0)
    g = []
    for field in range(fields):
        halo = jnp.where(paired, edges_pair[field], inner * edges_next[field])
        total = None
        for k, coef in enumerate(axial_coefs(), 1):
            after = jnp.where(slot + k >= EDGE, pltpu.roll(halo, LANES - k, 1), 0.0)
            before = jnp.where(slot - k < EDGE, pltpu.roll(halo, k, 1), 0.0)
            term = coef * jnp.where(slot < EDGE, after, -before)
            total = term if total is None else total + term
        g.append(total)
    u, rho, stiff, inverse = (flow_edges[i] for i in range(4))
    out = [
        u * g[0],
        u * g[1] + rho * g[0] + stiff * g[4],
        u * g[2],
        u * g[3],
        u * g[4] + inverse * g[1],
    ]
    for field in range(fields):
        fixes[field] = out[field]
    seen = jnp.concatenate([out[4] + out[1], jnp.zeros((TILE, LANES), jnp.float32)], axis=0)
    lines = jnp.dot(three_parts(seen), edge_column[...], preferred_element_type=jnp.float32)
    share = jnp.sum(edge_line[...] * add_parts(lines)[:TILE], axis=0, keepdims=True)
    spread = three_parts(owner[...] * (values[...] + share))
    totals[...] = add_parts(
        lax.dot_general(
            spread, place[...], (((1,), (1,)), ((), ())), preferred_element_type=jnp.float32
        )
    )


def store_body(held, fixes, totals, section, signal):
    sums = jnp.sum(totals[...], axis=0, keepdims=True)
    signal[...] = sums[0, : signal.shape[0]]
    fields, radial = section.shape[0], section.shape[2]
    lane = lax.broadcasted_iota(jnp.int32, (TILE, LANES), 1)
    outer = (lane < EDGE) | (lane >= LANES - EDGE)
    for field in range(fields):
        for row in range(0, radial, TILE):
            rows = pl.ds(row, TILE)
            fix = pltpu.roll(fixes[field], LANES - (SLOT * (row // TILE) + EDGE), 1)
            section[field, 0, rows, :] = held[field, 0, rows, :] + jnp.where(outer, fix, 0.0)


def in_vmem(count):
    return [pl.BlockSpec(memory_space=pltpu.VMEM)] * count


def in_smem(count):
    return [pl.BlockSpec(memory_space=pltpu.SMEM)] * count


def local(adjoint, density, velocity, pressure, fwh_cell, fwh_bin, fwh_weight, fwh_count):
    fields, local_theta, radial, axial_cells = adjoint.shape
    thetas, blocks_x = lax.axis_size("az"), lax.axis_size("rx")
    devices = thetas * blocks_x
    assert local_theta == 1 and axial_cells == LANES and blocks_x % 2 == 0
    assert thetas % 2 == 0 and thetas >= 6
    assert radial % TILE == 0 and radial // TILE * SLOT <= LANES
    params = pltpu.CompilerParams(vmem_limit_bytes=40 * 1024 * 1024)
    f32 = jnp.float32
    rows = fields * radial
    half, slots = rows // 2, fwh_cell.shape[2]
    edge_shape = jax.ShapeDtypeStruct((fields, TILE, LANES), f32)

    order = ring_order(thetas)
    onward = [(order[i], order[(i + 1) % thetas]) for i in range(thetas)]
    back = [(b, a) for a, b in onward]

    across = [(order[i], order[(i + thetas // 2) % thetas]) for i in range(thetas)]
    flat = adjoint.reshape(rows, LANES)
    own = [flat[:half], flat[half:]]
    steps = thetas // 2 - 1

    from_left, from_right, halves = list(own), list(own), []
    for step in range(steps):
        left, right = [], []
        for part in range(2):
            left.append(lax.ppermute(from_left[part], "az", onward))
            right.append(lax.ppermute(from_right[part], "az", back))
        from_left, from_right = left, right
        if step == 0:
            source, from_left[0] = lax.optimization_barrier((adjoint, from_left[0]))
            last_edges = pl.pallas_call(
                edges_body,
                out_shape=edge_shape,
                in_specs=in_vmem(1),
                out_specs=in_vmem(1)[0],
                compiler_params=params,
                name="edges",
            )(source)
            last_edges = lax.ppermute(last_edges, "az", across)
        if step == 0 + 1:
            last_edges, from_right[1] = lax.optimization_barrier((last_edges, from_right[1]))
        if step == 0:
            weights = lax.dynamic_slice_in_dim(
                jnp.asarray(ring_weights(thetas)), lax.axis_index("az"), 1, axis=0
            )
            tables = pl.pallas_call(
                slots_body,
                out_shape=(
                    jax.ShapeDtypeStruct((LANES, slots), jnp.bfloat16),
                    jax.ShapeDtypeStruct((radial, slots), f32),
                    jax.ShapeDtypeStruct((devices, slots), f32),
                    jax.ShapeDtypeStruct((LANES, slots), jnp.bfloat16),
                    jax.ShapeDtypeStruct((LANES, slots), jnp.bfloat16),
                    jax.ShapeDtypeStruct((TILE, slots), f32),
                    jax.ShapeDtypeStruct((4, TILE, LANES), f32),
                ),
                in_specs=in_smem(1) + in_vmem(6),
                out_specs=tuple(in_vmem(7)),
                compiler_params=params,
                name="slots",
            )(fwh_count, fwh_cell, fwh_bin, fwh_weight, density, velocity, pressure)
        if step == 1:
            weights, tables, from_right[1] = lax.optimization_barrier(
                (weights, tables, from_right[1])
            )
        if step == steps - 1:
            smooth, slope, spread, from_right[1] = lax.optimization_barrier(
                (smooth, slope, spread, from_right[1])
            )
            continue
        halves += from_left + from_right
        if step == steps - 2:
            smooth, slope, spread = pl.pallas_call(
                early_body,
                out_shape=(
                    jax.ShapeDtypeStruct((rows, LANES), f32),
                    jax.ShapeDtypeStruct((rows, LANES), f32),
                    jax.ShapeDtypeStruct((2 * thetas, TILE, LANES), f32),
                ),
                in_specs=in_smem(1) + in_vmem(1 + len(halves)),
                out_specs=tuple(in_vmem(3)),
                compiler_params=params,
                name="early",
            )(weights, adjoint, *halves)
    last_first = lax.ppermute(from_left[0], "az", onward)
    last_second = lax.ppermute(from_right[1], "az", back)

    smooth, slope, edges = pl.pallas_call(
        partial_body,
        out_shape=(jax.ShapeDtypeStruct((rows, LANES), f32),) * 2 + (edge_shape,),
        in_specs=in_vmem(8),
        out_specs=tuple(in_vmem(3)),
        compiler_params=params,
        name="partial",
    )(spread, smooth, slope, *from_left, *from_right, last_edges)
    pairs = [(b, b ^ 1) for b in range(blocks_x)]
    nexts = [(b, (b + (1 if b % 2 else -1)) % blocks_x) for b in range(blocks_x)]
    edges_next, edges_pair = lax.ppermute(edges, "rx", nexts), lax.ppermute(edges, "rx", pairs)
    place_x = jnp.reshape(lax.axis_index("rx"), (1, 1))

    column, line, owner, place, edge_column, edge_line, flow_edges = tables
    held, values = pl.pallas_call(
        bulk_body,
        out_shape=(
            jax.ShapeDtypeStruct(adjoint.shape, f32),
            jax.ShapeDtypeStruct((1, slots), f32),
        ),
        in_specs=in_vmem(10),
        out_specs=tuple(in_vmem(2)),
        scratch_shapes=[
            pltpu.VMEM((fields, radial + 2 * TILE, LANES), f32),
            pltpu.VMEM((radial, LANES), f32),
        ],
        compiler_params=params,
        name="bulk",
    )(
        spread,
        smooth,
        slope,
        last_first,
        last_second,
        density,
        velocity,
        pressure,
        column,
        line,
    )
    fixes, totals = pl.pallas_call(
        functools.partial(close_body, blocks_x),
        out_shape=(edge_shape, jax.ShapeDtypeStruct((devices, LANES), f32)),
        in_specs=in_smem(1) + in_vmem(8),
        out_specs=tuple(in_vmem(2)),
        compiler_params=params,
        name="close",
    )(
        place_x,
        edges_next,
        edges_pair,
        flow_edges,
        values,
        edge_column,
        edge_line,
        owner,
        place,
    )
    totals = lax.all_to_all(totals, ("az", "rx"), 0, 0, tiled=True)
    section, signal = pl.pallas_call(
        store_body,
        out_shape=(
            jax.ShapeDtypeStruct(adjoint.shape, f32),
            jax.ShapeDtypeStruct((BIN_DEV,), f32),
        ),
        in_specs=in_vmem(3),
        out_specs=tuple(in_vmem(2)),
        compiler_params=params,
        name="store",
    )(held, fixes, totals)
    return section, signal


def solution(mesh):
    placed = (
        P(None, "az", None, "rx"),
        P("az", None, "rx"),
        P(None, "az", None, "rx"),
        P("az", None, "rx"),
        P("az", "rx", None),
        P("az", "rx", None),
        P("az", "rx", None),
        P("az", "rx"),
    )
    return jax.shard_map(
        local,
        mesh=mesh,
        in_specs=placed,
        out_specs=(P(None, "az", None, "rx"), P(("az", "rx"))),
        check_vma=False,
    )
```

```python
import functools
import math

import jax
import jax.numpy as jnp
import numpy as np
from jax import lax
from jax.experimental import pallas as pl
from jax.experimental.pallas import tpu as pltpu
from jax.sharding import PartitionSpec as P

BIN_DEV = 8
LANES = 128
TILE = 8
EDGE = 3
SLOT = 8

ALPHA_FILTER = 0.495
COEF_ZERO = 11.0 / 16.0 + 5.0 * ALPHA_FILTER / 8.0
COEF_ONE = 15.0 / 32.0 + 17.0 * ALPHA_FILTER / 16.0
COEF_TWO = -3.0 / 16.0 + 3.0 * ALPHA_FILTER / 8.0
COEF_THREE = 1.0 / 32.0 - ALPHA_FILTER / 16.0
ALPHA_DERIV = 1.0 / 3.0
NEAR_COEF = 14.0 / 9.0
FAR_COEF = 1.0 / 9.0
AXIAL_STEP = 0.02
RADIAL_STEP = 0.02
INNER_RADIUS = 0.3
SECTION_STEP = 0.004
GAMMA_GAS = 1.4


def kernel_values(count):
    modes = np.arange(count)
    angle = modes * (2.0 * math.pi / count)
    cosine = np.cos(angle)
    filter_gain = (
        COEF_ZERO
        + COEF_ONE * cosine
        + COEF_TWO * np.cos(2.0 * angle)
        + COEF_THREE * np.cos(3.0 * angle)
    ) / (1.0 + 2.0 * ALPHA_FILTER * cosine)
    spacing = 2.0 * math.pi / count
    deriv_gain = (
        filter_gain
        * (NEAR_COEF * np.sin(angle) + 0.5 * FAR_COEF * np.sin(2.0 * angle))
        / (spacing * (1.0 + 2.0 * ALPHA_DERIV * cosine))
    )
    phase = np.mod(modes[:, None] * modes[None, :], count) * (2.0 * math.pi / count)
    smooth = np.sum(filter_gain * np.cos(phase), axis=-1) / count
    slope = -np.sum(deriv_gain * np.sin(phase), axis=-1) / count
    return smooth, slope


def ring_order(count):
    return list(range(0, count, 2)) + list(range(count - 1, 0, -2))


def ring_weights(count):
    order = ring_order(count)
    smooth, slope = kernel_values(count)
    rows = []
    for i in range(count):
        at = order.index(i)
        hops = [0]
        for s in range(1, count // 2):
            hops += [-s, s]
        hops.append(count // 2)
        away = [(i - order[(at + hop) % count]) % count for hop in hops]
        rows.append([smooth[d] for d in away] + [slope[d] for d in away])
    return np.array(rows, np.float32)


def packed_edges(tiles):
    lane = lax.broadcasted_iota(jnp.int32, (TILE, LANES), 1)
    packed = jnp.zeros((TILE, LANES), jnp.float32)
    for k, tile in enumerate(tiles):
        moved = pltpu.roll(tile, (SLOT * k + EDGE) % LANES, 1)
        packed = jnp.where(lax.shift_right_logical(lane, 3) == k, moved, packed)
    return packed


def edges_body(source, edges):
    fields, radial = source.shape[0], source.shape[2]
    for field in range(fields):
        tiles = [source[field, 0, pl.ds(row, TILE), :] for row in range(0, radial, TILE)]
        edges[field] = packed_edges(tiles)


def early_body(weights, source, *refs):
    count = weights.shape[1] // 2
    halves, (smooth, slope, spread) = refs[:-3], refs[-3:]
    for k in range(2 * count):
        spread[k] = jnp.full((TILE, LANES), weights[0, k], jnp.float32)
    fields, radial = source.shape[0], source.shape[2]
    half = halves[0].shape[0]
    for field in range(fields):
        for row in range(0, radial, TILE):
            at = field * radial + row
            value = source[field, 0, pl.ds(row, TILE), :]
            first, second = weights[0, 0] * value, weights[0, count] * value
            for k in range(len(halves) // 2):
                value = halves[2 * k + at // half][pl.ds(at % half, TILE), :]
                first = first + weights[0, 1 + k] * value
                second = second + weights[0, count + 1 + k] * value
            smooth[pl.ds(at, TILE), :] = first
            slope[pl.ds(at, TILE), :] = second


def partial_body(
    weights,
    early_smooth,
    early_slope,
    left_first,
    left_second,
    right_first,
    right_second,
    last_edges,
    smooth,
    slope,
    edges,
):
    count, fields = weights.shape[0] // 2, edges.shape[0]
    half, radial = left_first.shape[0], smooth.shape[0] // fields
    lefts, rights = (left_first, left_second), (right_first, right_second)
    for field in range(fields):
        tiles = []
        for row in range(0, radial, TILE):
            at = field * radial + row
            rows, part = pl.ds(at, TILE), pl.ds(at % half, TILE)
            left, right = lefts[at // half][part, :], rights[at // half][part, :]
            near, far = weights[count - 3], weights[count - 2]
            tiles.append(early_smooth[rows, :] + (near * left + far * right))
            smooth[rows, :] = tiles[-1]
            near, far = weights[2 * count - 3], weights[2 * count - 2]
            slope[rows, :] = early_slope[rows, :] + (near * left + far * right)
        edges[field] = packed_edges(tiles) + weights[count - 1] * last_edges[field]


def slots_body(
    blocks_x,
    live_count,
    place_x,
    cells,
    bins,
    slot_weights,
    density,
    velocity,
    pressure,
    column,
    line,
    owner,
    place,
    edge_column,
    edge_line,
    flow_edges,
    sides,
):
    slots, radial = cells.shape[2], density.shape[1]
    cell, own_bin = cells[0], bins[0]
    order = lax.broadcasted_iota(jnp.int32, (1, slots), 1)
    weight = jnp.where(order < live_count[0, 0], slot_weights[0], 0.0)
    x = cell & (LANES - 1)
    row = lax.shift_right_logical(cell, LANES.bit_length() - 1)

    def table(target, index, value):
        rows = lax.broadcasted_iota(jnp.int32, target.shape, 0)
        target[...] = jnp.where(rows == index, value, 0.0).astype(target.dtype)

    table(column, x, 1.0)
    table(line, row, weight)
    table(owner, own_bin // BIN_DEV, 1.0)
    table(place, own_bin % BIN_DEV, 1.0)
    base = SLOT * lax.shift_right_logical(row, TILE.bit_length() - 1)
    outer = jnp.where(x >= LANES - EDGE, base + (x - (LANES - EDGE)), -1)
    table(edge_column, jnp.where(x < EDGE, base + EDGE + x, outer), 1.0)
    table(edge_line, row & (TILE - 1), weight)
    for which, make in enumerate(
        (
            lambda rows: velocity[0, 0, rows, :],
            lambda rows: density[0, rows, :],
            lambda rows: GAMMA_GAS * pressure[0, rows, :],
            lambda rows: 1.0 / density[0, rows, :],
        )
    ):
        tiles = [make(pl.ds(at, TILE)) for at in range(0, radial, TILE)]
        flow_edges[which] = packed_edges(tiles)
    slot = lax.broadcasted_iota(jnp.int32, (TILE, LANES), 1) & (SLOT - 1)
    paired = (slot < EDGE) == ((place_x[0, 0] & 1) == 1)
    inner = jnp.where((place_x[0, 0] == 0) | (place_x[0, 0] == blocks_x - 1), 0.0, 1.0)
    sides[0] = jnp.where(paired, 1.0, 0.0)
    sides[1] = jnp.where(paired, 0.0, inner)


def three_parts(value):
    parts = []
    for _ in range(3):
        part = value.astype(jnp.bfloat16)
        parts.append(part)
        value = value - part.astype(jnp.float32)
    return jnp.concatenate(parts, axis=0)


def add_parts(stacked):
    rows = stacked.shape[0] // 3
    return stacked[:rows] + (stacked[rows : 2 * rows] + stacked[2 * rows :])


def axial_coefs():
    unit = SECTION_STEP / (60.0 * AXIAL_STEP)
    return [np.float32(c * unit) for c in (45.0, -9.0, 1.0)]


def bulk_body(
    weights,
    smooth,
    slope,
    last_first,
    last_second,
    density,
    velocity,
    pressure,
    column,
    line,
    section,
    values,
    filtered,
    picked,
):
    fields, radial = section.shape[0], section.shape[2]
    count = weights.shape[0] // 2
    half = last_first.shape[0]
    last_weight, last_slope = weights[count - 1], weights[2 * count - 1]

    def last(at):
        source = last_first if at < half else last_second
        return source[pl.ds(at % half, TILE), :]

    lane = lax.broadcasted_iota(jnp.int32, (TILE, LANES), 1)
    sub = lax.broadcasted_iota(jnp.int32, (TILE, LANES), 0)
    pad = jnp.zeros((TILE, LANES), jnp.float32)
    for field in range(fields):
        filtered[field, pl.ds(0, TILE), :] = pad
        filtered[field, pl.ds(TILE + radial, TILE), :] = pad
        for row in range(0, radial, TILE):
            at = field * radial + row
            value = smooth[pl.ds(at, TILE), :] + last_weight * last(at)
            filtered[field, pl.ds(TILE + row, TILE), :] = value

    axial = axial_coefs()
    unit = SECTION_STEP / (60.0 * RADIAL_STEP)
    radially = [np.float32(c * unit) for c in (45.0, -9.0, 1.0)]

    for row in range(0, radial, TILE):
        rows = pl.ds(row, TILE)
        middle, g, e, s = [], [], [], []
        cell_radius = INNER_RADIUS + ((sub + row).astype(jnp.float32) + 0.5) * RADIAL_STEP
        stretch = SECTION_STEP / cell_radius
        for field in range(fields):
            here = filtered[field, pl.ds(TILE + row, TILE), :]
            total = None
            for k in range(1, EDGE + 1):
                ahead = pltpu.roll(jnp.where(lane < k, 0.0, here), LANES - k, 1)
                behind = pltpu.roll(jnp.where(lane >= LANES - k, 0.0, here), k, 1)
                term = axial[k - 1] * (ahead - behind)
                total = term if total is None else total + term
            g.append(total)
            total = None
            for k in range(1, EDGE + 1):
                above = filtered[field, pl.ds(TILE + row + k, TILE), :]
                below = filtered[field, pl.ds(TILE + row - k, TILE), :]
                term = radially[k - 1] * (above - below)
                total = term if total is None else total + term
            e.append(total)
            at = field * radial + row
            s.append((slope[pl.ds(at, TILE), :] + last_slope * last(at)) * stretch)
            middle.append(here)
        rho = density[0, rows, :]
        u, v, w = (velocity[i, 0, rows, :] for i in range(3))
        stiff = GAMMA_GAS * pressure[0, rows, :]
        inverse = 1.0 / rho
        moved = [u * g[i] + v * e[i] + w * s[i] for i in range(fields)]
        out = [
            middle[0] + moved[0],
            middle[1] + (moved[1] + rho * g[0] + stiff * g[4]),
            middle[2] + (moved[2] + rho * e[0] + stiff * e[4]),
            middle[3] + (moved[3] + rho * s[0] + stiff * s[4]),
            middle[4] + (moved[4] + inverse * (g[1] + e[2] + s[3])),
        ]
        for field in range(fields):
            section[field, 0, rows, :] = out[field]
        picked[rows, :] = out[4] + out[1]

    lines = jnp.dot(three_parts(picked[...]), column[...], preferred_element_type=jnp.float32)
    values[...] = jnp.sum(line[...] * add_parts(lines), axis=0, keepdims=True)


def close_body(
    sides,
    edges_next,
    edges_pair,
    flow_edges,
    values,
    edge_column,
    edge_line,
    owner,
    place,
    fixes,
    totals,
):
    fields = fixes.shape[0]
    lane = lax.broadcasted_iota(jnp.int32, (TILE, LANES), 1)
    slot = lane & (SLOT - 1)
    g = []
    for field in range(fields):
        halo = sides[0] * edges_pair[field] + sides[1] * edges_next[field]
        total = None
        for k, coef in enumerate(axial_coefs(), 1):
            after = jnp.where(slot + k >= EDGE, pltpu.roll(halo, LANES - k, 1), 0.0)
            before = jnp.where(slot - k < EDGE, pltpu.roll(halo, k, 1), 0.0)
            term = coef * jnp.where(slot < EDGE, after, -before)
            total = term if total is None else total + term
        g.append(total)
    u, rho, stiff, inverse = (flow_edges[i] for i in range(4))
    out = [
        u * g[0],
        u * g[1] + rho * g[0] + stiff * g[4],
        u * g[2],
        u * g[3],
        u * g[4] + inverse * g[1],
    ]
    for field in range(fields):
        fixes[field] = out[field]
    seen = jnp.concatenate([out[4] + out[1], jnp.zeros((TILE, LANES), jnp.float32)], axis=0)
    lines = jnp.dot(three_parts(seen), edge_column[...], preferred_element_type=jnp.float32)
    share = jnp.sum(edge_line[...] * add_parts(lines)[:TILE], axis=0, keepdims=True)
    spread = three_parts(owner[...] * (values[...] + share))
    totals[...] = add_parts(
        lax.dot_general(
            spread, place[...], (((1,), (1,)), ((), ())), preferred_element_type=jnp.float32
        )
    )


def store_body(held, fixes, totals, section, signal):
    sums = jnp.sum(totals[...], axis=0, keepdims=True)
    signal[...] = sums[0, : signal.shape[0]]
    fields, radial = section.shape[0], section.shape[2]
    lane = lax.broadcasted_iota(jnp.int32, (TILE, LANES), 1)
    outer = (lane < EDGE) | (lane >= LANES - EDGE)
    for field in range(fields):
        for row in range(0, radial, TILE):
            rows = pl.ds(row, TILE)
            fix = pltpu.roll(fixes[field], LANES - (SLOT * (row // TILE) + EDGE), 1)
            section[field, 0, rows, :] = held[field, 0, rows, :] + jnp.where(outer, fix, 0.0)


def in_vmem(count):
    return [pl.BlockSpec(memory_space=pltpu.VMEM)] * count


def in_smem(count):
    return [pl.BlockSpec(memory_space=pltpu.SMEM)] * count


def local(adjoint, density, velocity, pressure, fwh_cell, fwh_bin, fwh_weight, fwh_count):
    fields, local_theta, radial, axial_cells = adjoint.shape
    thetas, blocks_x = lax.axis_size("az"), lax.axis_size("rx")
    devices = thetas * blocks_x
    assert local_theta == 1 and axial_cells == LANES and blocks_x % 2 == 0
    assert thetas % 2 == 0 and thetas >= 6
    assert radial % TILE == 0 and radial // TILE * SLOT <= LANES
    params = pltpu.CompilerParams(vmem_limit_bytes=40 * 1024 * 1024)
    f32 = jnp.float32
    rows = fields * radial
    half, slots = rows // 2, fwh_cell.shape[2]
    edge_shape = jax.ShapeDtypeStruct((fields, TILE, LANES), f32)

    order = ring_order(thetas)
    onward = [(order[i], order[(i + 1) % thetas]) for i in range(thetas)]
    back = [(b, a) for a, b in onward]

    across = [(order[i], order[(i + thetas // 2) % thetas]) for i in range(thetas)]
    place_x = jnp.reshape(lax.axis_index("rx"), (1, 1))
    flat = adjoint.reshape(rows, LANES)
    own = [flat[:half], flat[half:]]
    steps = thetas // 2 - 1

    from_left, from_right, halves = list(own), list(own), []
    for step in range(steps):
        left, right = [], []
        for part in range(2):
            left.append(lax.ppermute(from_left[part], "az", onward))
            right.append(lax.ppermute(from_right[part], "az", back))
        from_left, from_right = left, right
        if step == 0:
            source, from_left[0] = lax.optimization_barrier((adjoint, from_left[0]))
            last_edges = pl.pallas_call(
                edges_body,
                out_shape=edge_shape,
                in_specs=in_vmem(1),
                out_specs=in_vmem(1)[0],
                compiler_params=params,
                name="edges",
            )(source)
            last_edges = lax.ppermute(last_edges, "az", across)
        if step == 0 + 1:
            last_edges, from_right[1] = lax.optimization_barrier((last_edges, from_right[1]))
        if step == 0:
            weights = lax.dynamic_slice_in_dim(
                jnp.asarray(ring_weights(thetas)), lax.axis_index("az"), 1, axis=0
            )
            tables = pl.pallas_call(
                functools.partial(slots_body, blocks_x),
                out_shape=(
                    jax.ShapeDtypeStruct((LANES, slots), jnp.bfloat16),
                    jax.ShapeDtypeStruct((radial, slots), f32),
                    jax.ShapeDtypeStruct((devices, slots), f32),
                    jax.ShapeDtypeStruct((LANES, slots), jnp.bfloat16),
                    jax.ShapeDtypeStruct((LANES, slots), jnp.bfloat16),
                    jax.ShapeDtypeStruct((TILE, slots), f32),
                    jax.ShapeDtypeStruct((4, TILE, LANES), f32),
                    jax.ShapeDtypeStruct((2, TILE, LANES), f32),
                ),
                in_specs=in_smem(2) + in_vmem(6),
                out_specs=tuple(in_vmem(8)),
                compiler_params=params,
                name="slots",
            )(fwh_count, place_x, fwh_cell, fwh_bin, fwh_weight, density, velocity, pressure)
        if step == 1:
            weights, tables, from_right[1] = lax.optimization_barrier(
                (weights, tables, from_right[1])
            )
        if step == steps - 1:
            smooth, slope, spread, from_right[1] = lax.optimization_barrier(
                (smooth, slope, spread, from_right[1])
            )
            continue
        halves += from_left + from_right
        if step == steps - 2:
            smooth, slope, spread = pl.pallas_call(
                early_body,
                out_shape=(
                    jax.ShapeDtypeStruct((rows, LANES), f32),
                    jax.ShapeDtypeStruct((rows, LANES), f32),
                    jax.ShapeDtypeStruct((2 * thetas, TILE, LANES), f32),
                ),
                in_specs=in_smem(1) + in_vmem(1 + len(halves)),
                out_specs=tuple(in_vmem(3)),
                compiler_params=params,
                name="early",
            )(weights, adjoint, *halves)
    last_first = lax.ppermute(from_left[0], "az", onward)
    last_second = lax.ppermute(from_right[1], "az", back)

    smooth, slope, edges = pl.pallas_call(
        partial_body,
        out_shape=(jax.ShapeDtypeStruct((rows, LANES), f32),) * 2 + (edge_shape,),
        in_specs=in_vmem(8),
        out_specs=tuple(in_vmem(3)),
        compiler_params=params,
        name="partial",
    )(spread, smooth, slope, *from_left, *from_right, last_edges)
    pairs = [(b, b ^ 1) for b in range(blocks_x)]
    nexts = [(b, (b + (1 if b % 2 else -1)) % blocks_x) for b in range(blocks_x)]
    edges_next, edges_pair = lax.ppermute(edges, "rx", nexts), lax.ppermute(edges, "rx", pairs)

    column, line, owner, place, edge_column, edge_line, flow_edges, sides = tables
    held, values = pl.pallas_call(
        bulk_body,
        out_shape=(
            jax.ShapeDtypeStruct(adjoint.shape, f32),
            jax.ShapeDtypeStruct((1, slots), f32),
        ),
        in_specs=in_vmem(10),
        out_specs=tuple(in_vmem(2)),
        scratch_shapes=[
            pltpu.VMEM((fields, radial + 2 * TILE, LANES), f32),
            pltpu.VMEM((radial, LANES), f32),
        ],
        compiler_params=params,
        name="bulk",
    )(
        spread,
        smooth,
        slope,
        last_first,
        last_second,
        density,
        velocity,
        pressure,
        column,
        line,
    )
    fixes, totals = pl.pallas_call(
        close_body,
        out_shape=(edge_shape, jax.ShapeDtypeStruct((devices, LANES), f32)),
        in_specs=in_vmem(9),
        out_specs=tuple(in_vmem(2)),
        compiler_params=params,
        name="close",
    )(
        sides,
        edges_next,
        edges_pair,
        flow_edges,
        values,
        edge_column,
        edge_line,
        owner,
        place,
    )
    totals = lax.all_to_all(totals, ("az", "rx"), 0, 0, tiled=True)
    section, signal = pl.pallas_call(
        store_body,
        out_shape=(
            jax.ShapeDtypeStruct(adjoint.shape, f32),
            jax.ShapeDtypeStruct((BIN_DEV,), f32),
        ),
        in_specs=in_vmem(3),
        out_specs=tuple(in_vmem(2)),
        compiler_params=params,
        name="store",
    )(held, fixes, totals)
    return section, signal


def solution(mesh):
    placed = (
        P(None, "az", None, "rx"),
        P("az", None, "rx"),
        P(None, "az", None, "rx"),
        P("az", None, "rx"),
        P("az", "rx", None),
        P("az", "rx", None),
        P("az", "rx", None),
        P("az", "rx"),
    )
    return jax.shard_map(
        local,
        mesh=mesh,
        in_specs=placed,
        out_specs=(P(None, "az", None, "rx"), P(("az", "rx"))),
        check_vma=False,
    )
```

```python
import functools
import math

import jax
import jax.numpy as jnp
import numpy as np
from jax import lax
from jax.experimental import pallas as pl
from jax.experimental.pallas import tpu as pltpu
from jax.sharding import PartitionSpec as P

BIN_DEV = 8
LANES = 128
TILE = 8
EDGE = 3
SLOT = 8

ALPHA_FILTER = 0.495
COEF_ZERO = 11.0 / 16.0 + 5.0 * ALPHA_FILTER / 8.0
COEF_ONE = 15.0 / 32.0 + 17.0 * ALPHA_FILTER / 16.0
COEF_TWO = -3.0 / 16.0 + 3.0 * ALPHA_FILTER / 8.0
COEF_THREE = 1.0 / 32.0 - ALPHA_FILTER / 16.0
ALPHA_DERIV = 1.0 / 3.0
NEAR_COEF = 14.0 / 9.0
FAR_COEF = 1.0 / 9.0
AXIAL_STEP = 0.02
RADIAL_STEP = 0.02
INNER_RADIUS = 0.3
SECTION_STEP = 0.004
GAMMA_GAS = 1.4


def kernel_values(count):
    modes = np.arange(count)
    angle = modes * (2.0 * math.pi / count)
    cosine = np.cos(angle)
    filter_gain = (
        COEF_ZERO
        + COEF_ONE * cosine
        + COEF_TWO * np.cos(2.0 * angle)
        + COEF_THREE * np.cos(3.0 * angle)
    ) / (1.0 + 2.0 * ALPHA_FILTER * cosine)
    spacing = 2.0 * math.pi / count
    deriv_gain = (
        filter_gain
        * (NEAR_COEF * np.sin(angle) + 0.5 * FAR_COEF * np.sin(2.0 * angle))
        / (spacing * (1.0 + 2.0 * ALPHA_DERIV * cosine))
    )
    phase = np.mod(modes[:, None] * modes[None, :], count) * (2.0 * math.pi / count)
    smooth = np.sum(filter_gain * np.cos(phase), axis=-1) / count
    slope = -np.sum(deriv_gain * np.sin(phase), axis=-1) / count
    return smooth, slope


def ring_order(count):
    return list(range(0, count, 2)) + list(range(count - 1, 0, -2))


def ring_weights(count):
    order = ring_order(count)
    smooth, slope = kernel_values(count)
    rows = []
    for i in range(count):
        at = order.index(i)
        hops = [0]
        for s in range(1, count // 2):
            hops += [-s, s]
        hops.append(count // 2)
        away = [(i - order[(at + hop) % count]) % count for hop in hops]
        rows.append([smooth[d] for d in away] + [slope[d] for d in away])
    return np.array(rows, np.float32)


def packed_edges(tiles):
    lane = lax.broadcasted_iota(jnp.int32, (TILE, LANES), 1)
    packed = jnp.zeros((TILE, LANES), jnp.float32)
    for k, tile in enumerate(tiles):
        moved = pltpu.roll(tile, (SLOT * k + EDGE) % LANES, 1)
        packed = jnp.where(lax.shift_right_logical(lane, 3) == k, moved, packed)
    return packed


def edges_body(first, second, edges):
    fields, half = edges.shape[0], first.shape[0]
    radial = 2 * half // fields
    for field in range(fields):
        places = range(field * radial, (field + 1) * radial, TILE)
        tiles = [(first if at < half else second)[pl.ds(at % half, TILE), :] for at in places]
        edges[field] = packed_edges(tiles)


def early_body(weights, *refs):
    count = weights.shape[1] // 2
    halves, (smooth, slope, spread) = refs[:-3], refs[-3:]
    for k in range(2 * count):
        spread[k] = jnp.full((TILE, LANES), weights[0, k], jnp.float32)
    half = halves[0].shape[0]
    for at in range(0, 2 * half, TILE):
        first = second = None
        for k in range(len(halves) // 2):
            value = halves[2 * k + at // half][pl.ds(at % half, TILE), :]
            terms = weights[0, k] * value, weights[0, count + k] * value
            first = terms[0] if first is None else first + terms[0]
            second = terms[1] if second is None else second + terms[1]
        smooth[pl.ds(at, TILE), :] = first
        slope[pl.ds(at, TILE), :] = second


def partial_body(
    weights,
    early_smooth,
    early_slope,
    left_first,
    left_second,
    right_first,
    right_second,
    last_edges,
    smooth,
    slope,
    edges,
):
    count, fields = weights.shape[0] // 2, edges.shape[0]
    half, radial = left_first.shape[0], smooth.shape[0] // fields
    lefts, rights = (left_first, left_second), (right_first, right_second)
    for field in range(fields):
        tiles = []
        for row in range(0, radial, TILE):
            at = field * radial + row
            rows, part = pl.ds(at, TILE), pl.ds(at % half, TILE)
            left, right = lefts[at // half][part, :], rights[at // half][part, :]
            near, far = weights[count - 3], weights[count - 2]
            tiles.append(early_smooth[rows, :] + (near * left + far * right))
            smooth[rows, :] = tiles[-1]
            near, far = weights[2 * count - 3], weights[2 * count - 2]
            slope[rows, :] = early_slope[rows, :] + (near * left + far * right)
        edges[field] = packed_edges(tiles) + weights[count - 1] * last_edges[field]


def slots_body(
    blocks_x,
    live_count,
    place_x,
    cells,
    bins,
    slot_weights,
    density,
    velocity,
    pressure,
    column,
    line,
    owner,
    place,
    edge_column,
    edge_line,
    flow_edges,
    sides,
):
    slots, radial = cells.shape[2], density.shape[1]
    cell, own_bin = cells[0], bins[0]
    order = lax.broadcasted_iota(jnp.int32, (1, slots), 1)
    weight = jnp.where(order < live_count[0, 0], slot_weights[0], 0.0)
    x = cell & (LANES - 1)
    row = lax.shift_right_logical(cell, LANES.bit_length() - 1)

    def table(target, index, value):
        rows = lax.broadcasted_iota(jnp.int32, target.shape, 0)
        target[...] = jnp.where(rows == index, value, 0.0).astype(target.dtype)

    table(column, x, 1.0)
    table(line, row, weight)
    table(owner, own_bin // BIN_DEV, 1.0)
    table(place, own_bin % BIN_DEV, 1.0)
    base = SLOT * lax.shift_right_logical(row, TILE.bit_length() - 1)
    outer = jnp.where(x >= LANES - EDGE, base + (x - (LANES - EDGE)), -1)
    table(edge_column, jnp.where(x < EDGE, base + EDGE + x, outer), 1.0)
    table(edge_line, row & (TILE - 1), weight)
    for which, make in enumerate(
        (
            lambda rows: velocity[0, 0, rows, :],
            lambda rows: density[0, rows, :],
            lambda rows: GAMMA_GAS * pressure[0, rows, :],
            lambda rows: 1.0 / density[0, rows, :],
        )
    ):
        tiles = [make(pl.ds(at, TILE)) for at in range(0, radial, TILE)]
        flow_edges[which] = packed_edges(tiles)
    slot = lax.broadcasted_iota(jnp.int32, (TILE, LANES), 1) & (SLOT - 1)
    paired = (slot < EDGE) == ((place_x[0, 0] & 1) == 1)
    inner = jnp.where((place_x[0, 0] == 0) | (place_x[0, 0] == blocks_x - 1), 0.0, 1.0)
    sides[0] = jnp.where(paired, 1.0, 0.0)
    sides[1] = jnp.where(paired, 0.0, inner)


def three_parts(value):
    parts = []
    for _ in range(3):
        part = value.astype(jnp.bfloat16)
        parts.append(part)
        value = value - part.astype(jnp.float32)
    return jnp.concatenate(parts, axis=0)


def add_parts(stacked):
    rows = stacked.shape[0] // 3
    return stacked[:rows] + (stacked[rows : 2 * rows] + stacked[2 * rows :])


def axial_coefs():
    unit = SECTION_STEP / (60.0 * AXIAL_STEP)
    return [np.float32(c * unit) for c in (45.0, -9.0, 1.0)]


def bulk_body(
    weights,
    smooth,
    slope,
    last_first,
    last_second,
    density,
    velocity,
    pressure,
    column,
    line,
    section,
    values,
    filtered,
    picked,
):
    fields, radial = section.shape[0], section.shape[2]
    count = weights.shape[0] // 2
    half = last_first.shape[0]
    last_weight, last_slope = weights[count - 1], weights[2 * count - 1]

    def last(at):
        source = last_first if at < half else last_second
        return source[pl.ds(at % half, TILE), :]

    lane = lax.broadcasted_iota(jnp.int32, (TILE, LANES), 1)
    sub = lax.broadcasted_iota(jnp.int32, (TILE, LANES), 0)
    pad = jnp.zeros((TILE, LANES), jnp.float32)
    for field in range(fields):
        filtered[field, pl.ds(0, TILE), :] = pad
        filtered[field, pl.ds(TILE + radial, TILE), :] = pad
        for row in range(0, radial, TILE):
            at = field * radial + row
            value = smooth[pl.ds(at, TILE), :] + last_weight * last(at)
            filtered[field, pl.ds(TILE + row, TILE), :] = value

    axial = axial_coefs()
    unit = SECTION_STEP / (60.0 * RADIAL_STEP)
    radially = [np.float32(c * unit) for c in (45.0, -9.0, 1.0)]

    for row in range(0, radial, TILE):
        rows = pl.ds(row, TILE)
        middle, g, e, s = [], [], [], []
        cell_radius = INNER_RADIUS + ((sub + row).astype(jnp.float32) + 0.5) * RADIAL_STEP
        stretch = SECTION_STEP / cell_radius
        for field in range(fields):
            here = filtered[field, pl.ds(TILE + row, TILE), :]
            total = None
            for k in range(1, EDGE + 1):
                ahead = pltpu.roll(jnp.where(lane < k, 0.0, here), LANES - k, 1)
                behind = pltpu.roll(jnp.where(lane >= LANES - k, 0.0, here), k, 1)
                term = axial[k - 1] * (ahead - behind)
                total = term if total is None else total + term
            g.append(total)
            total = None
            for k in range(1, EDGE + 1):
                above = filtered[field, pl.ds(TILE + row + k, TILE), :]
                below = filtered[field, pl.ds(TILE + row - k, TILE), :]
                term = radially[k - 1] * (above - below)
                total = term if total is None else total + term
            e.append(total)
            at = field * radial + row
            s.append((slope[pl.ds(at, TILE), :] + last_slope * last(at)) * stretch)
            middle.append(here)
        rho = density[0, rows, :]
        u, v, w = (velocity[i, 0, rows, :] for i in range(3))
        stiff = GAMMA_GAS * pressure[0, rows, :]
        inverse = 1.0 / rho
        moved = [u * g[i] + v * e[i] + w * s[i] for i in range(fields)]
        out = [
            middle[0] + moved[0],
            middle[1] + (moved[1] + rho * g[0] + stiff * g[4]),
            middle[2] + (moved[2] + rho * e[0] + stiff * e[4]),
            middle[3] + (moved[3] + rho * s[0] + stiff * s[4]),
            middle[4] + (moved[4] + inverse * (g[1] + e[2] + s[3])),
        ]
        for field in range(fields):
            section[field, 0, rows, :] = out[field]
        picked[rows, :] = out[4] + out[1]

    lines = jnp.dot(three_parts(picked[...]), column[...], preferred_element_type=jnp.float32)
    values[...] = jnp.sum(line[...] * add_parts(lines), axis=0, keepdims=True)


def close_body(
    sides,
    edges_next,
    edges_pair,
    flow_edges,
    values,
    edge_column,
    edge_line,
    owner,
    place,
    fixes,
    totals,
):
    fields = fixes.shape[0]
    lane = lax.broadcasted_iota(jnp.int32, (TILE, LANES), 1)
    slot = lane & (SLOT - 1)
    g = []
    for field in range(fields):
        halo = sides[0] * edges_pair[field] + sides[1] * edges_next[field]
        total = None
        for k, coef in enumerate(axial_coefs(), 1):
            after = jnp.where(slot + k >= EDGE, pltpu.roll(halo, LANES - k, 1), 0.0)
            before = jnp.where(slot - k < EDGE, pltpu.roll(halo, k, 1), 0.0)
            term = coef * jnp.where(slot < EDGE, after, -before)
            total = term if total is None else total + term
        g.append(total)
    u, rho, stiff, inverse = (flow_edges[i] for i in range(4))
    out = [
        u * g[0],
        u * g[1] + rho * g[0] + stiff * g[4],
        u * g[2],
        u * g[3],
        u * g[4] + inverse * g[1],
    ]
    for field in range(fields):
        fixes[field] = out[field]
    seen = jnp.concatenate([out[4] + out[1], jnp.zeros((TILE, LANES), jnp.float32)], axis=0)
    lines = jnp.dot(three_parts(seen), edge_column[...], preferred_element_type=jnp.float32)
    share = jnp.sum(edge_line[...] * add_parts(lines)[:TILE], axis=0, keepdims=True)
    spread = three_parts(owner[...] * (values[...] + share))
    totals[...] = add_parts(
        lax.dot_general(
            spread, place[...], (((1,), (1,)), ((), ())), preferred_element_type=jnp.float32
        )
    )


def store_body(held, fixes, totals, section, signal):
    sums = jnp.sum(totals[...], axis=0, keepdims=True)
    signal[...] = sums[0, : signal.shape[0]]
    fields, radial = section.shape[0], section.shape[2]
    lane = lax.broadcasted_iota(jnp.int32, (TILE, LANES), 1)
    outer = (lane < EDGE) | (lane >= LANES - EDGE)
    for field in range(fields):
        for row in range(0, radial, TILE):
            rows = pl.ds(row, TILE)
            fix = pltpu.roll(fixes[field], LANES - (SLOT * (row // TILE) + EDGE), 1)
            section[field, 0, rows, :] = held[field, 0, rows, :] + jnp.where(outer, fix, 0.0)


def in_vmem(count):
    return [pl.BlockSpec(memory_space=pltpu.VMEM)] * count


def in_smem(count):
    return [pl.BlockSpec(memory_space=pltpu.SMEM)] * count


def local(adjoint, density, velocity, pressure, fwh_cell, fwh_bin, fwh_weight, fwh_count):
    fields, local_theta, radial, axial_cells = adjoint.shape
    thetas, blocks_x = lax.axis_size("az"), lax.axis_size("rx")
    devices = thetas * blocks_x
    assert local_theta == 1 and axial_cells == LANES and blocks_x % 2 == 0
    assert thetas % 2 == 0 and thetas >= 6
    assert radial % TILE == 0 and radial // TILE * SLOT <= LANES
    params = pltpu.CompilerParams(vmem_limit_bytes=40 * 1024 * 1024)
    f32 = jnp.float32
    rows = fields * radial
    half, slots = rows // 2, fwh_cell.shape[2]
    edge_shape = jax.ShapeDtypeStruct((fields, TILE, LANES), f32)

    order = ring_order(thetas)
    onward = [(order[i], order[(i + 1) % thetas]) for i in range(thetas)]
    back = [(b, a) for a, b in onward]

    across = [(order[i], order[(i + thetas // 2) % thetas]) for i in range(thetas)]
    place_x = jnp.reshape(lax.axis_index("rx"), (1, 1))
    flat = adjoint.reshape(rows, LANES)
    own = [flat[:half], flat[half:]]
    steps = thetas // 2 - 1

    from_left, from_right, halves = list(own), list(own), []
    for step in range(steps):
        left, right = [], []
        for part in range(2):
            left.append(lax.ppermute(from_left[part], "az", onward))
            right.append(lax.ppermute(from_right[part], "az", back))
        from_left, from_right = left, right
        if step == 0:
            source, from_left[0] = lax.optimization_barrier((own[1], from_left[0]))
            last_edges = pl.pallas_call(
                edges_body,
                out_shape=edge_shape,
                in_specs=in_vmem(2),
                out_specs=in_vmem(1)[0],
                compiler_params=params,
                name="edges",
            )(own[0], source)
            last_edges = lax.ppermute(last_edges, "az", across)
        if step == 0 + 1:
            last_edges, from_right[1] = lax.optimization_barrier((last_edges, from_right[1]))
        if step == 0:
            weights = lax.dynamic_slice_in_dim(
                jnp.asarray(ring_weights(thetas)), lax.axis_index("az"), 1, axis=0
            )
            tables = pl.pallas_call(
                functools.partial(slots_body, blocks_x),
                out_shape=(
                    jax.ShapeDtypeStruct((LANES, slots), jnp.bfloat16),
                    jax.ShapeDtypeStruct((radial, slots), f32),
                    jax.ShapeDtypeStruct((devices, slots), f32),
                    jax.ShapeDtypeStruct((LANES, slots), jnp.bfloat16),
                    jax.ShapeDtypeStruct((LANES, slots), jnp.bfloat16),
                    jax.ShapeDtypeStruct((TILE, slots), f32),
                    jax.ShapeDtypeStruct((4, TILE, LANES), f32),
                    jax.ShapeDtypeStruct((2, TILE, LANES), f32),
                ),
                in_specs=in_smem(2) + in_vmem(6),
                out_specs=tuple(in_vmem(8)),
                compiler_params=params,
                name="slots",
            )(fwh_count, place_x, fwh_cell, fwh_bin, fwh_weight, density, velocity, pressure)
        if step == 1:
            weights, tables, from_right[1] = lax.optimization_barrier(
                (weights, tables, from_right[1])
            )
        if step == steps - 1:
            smooth, slope, spread, from_right[1] = lax.optimization_barrier(
                (smooth, slope, spread, from_right[1])
            )
            continue
        halves += from_left + from_right
        if step == steps - 2:
            smooth, slope, spread = pl.pallas_call(
                early_body,
                out_shape=(
                    jax.ShapeDtypeStruct((rows, LANES), f32),
                    jax.ShapeDtypeStruct((rows, LANES), f32),
                    jax.ShapeDtypeStruct((2 * thetas, TILE, LANES), f32),
                ),
                in_specs=in_smem(1) + in_vmem(2 + len(halves)),
                out_specs=tuple(in_vmem(3)),
                compiler_params=params,
                name="early",
            )(weights, *own, *halves)
    last_first = lax.ppermute(from_left[0], "az", onward)
    last_second = lax.ppermute(from_right[1], "az", back)

    smooth, slope, edges = pl.pallas_call(
        partial_body,
        out_shape=(jax.ShapeDtypeStruct((rows, LANES), f32),) * 2 + (edge_shape,),
        in_specs=in_vmem(8),
        out_specs=tuple(in_vmem(3)),
        compiler_params=params,
        name="partial",
    )(spread, smooth, slope, *from_left, *from_right, last_edges)
    pairs = [(b, b ^ 1) for b in range(blocks_x)]
    nexts = [(b, (b + (1 if b % 2 else -1)) % blocks_x) for b in range(blocks_x)]
    edges_next, edges_pair = lax.ppermute(edges, "rx", nexts), lax.ppermute(edges, "rx", pairs)

    column, line, owner, place, edge_column, edge_line, flow_edges, sides = tables
    held, values = pl.pallas_call(
        bulk_body,
        out_shape=(
            jax.ShapeDtypeStruct(adjoint.shape, f32),
            jax.ShapeDtypeStruct((1, slots), f32),
        ),
        in_specs=in_vmem(10),
        out_specs=tuple(in_vmem(2)),
        scratch_shapes=[
            pltpu.VMEM((fields, radial + 2 * TILE, LANES), f32),
            pltpu.VMEM((radial, LANES), f32),
        ],
        compiler_params=params,
        name="bulk",
    )(
        spread,
        smooth,
        slope,
        last_first,
        last_second,
        density,
        velocity,
        pressure,
        column,
        line,
    )
    fixes, totals = pl.pallas_call(
        close_body,
        out_shape=(edge_shape, jax.ShapeDtypeStruct((devices, LANES), f32)),
        in_specs=in_vmem(9),
        out_specs=tuple(in_vmem(2)),
        compiler_params=params,
        name="close",
    )(
        sides,
        edges_next,
        edges_pair,
        flow_edges,
        values,
        edge_column,
        edge_line,
        owner,
        place,
    )
    totals = lax.all_to_all(totals, ("az", "rx"), 0, 0, tiled=True)
    section, signal = pl.pallas_call(
        store_body,
        out_shape=(
            jax.ShapeDtypeStruct(adjoint.shape, f32),
            jax.ShapeDtypeStruct((BIN_DEV,), f32),
        ),
        in_specs=in_vmem(3),
        out_specs=tuple(in_vmem(2)),
        compiler_params=params,
        name="store",
    )(held, fixes, totals)
    return section, signal


def solution(mesh):
    placed = (
        P(None, "az", None, "rx"),
        P("az", None, "rx"),
        P(None, "az", None, "rx"),
        P("az", None, "rx"),
        P("az", "rx", None),
        P("az", "rx", None),
        P("az", "rx", None),
        P("az", "rx"),
    )
    return jax.shard_map(
        local,
        mesh=mesh,
        in_specs=placed,
        out_specs=(P(None, "az", None, "rx"), P(("az", "rx"))),
        check_vma=False,
    )
```
